32 devices in a mesh: dp: 4 (over z), expert: 8 (over y, x, core).
Axes of the slice: x: 2, y: 2, z: 4, core: 2. Of those that a mesh axis runs over, the one named last changes fastest.
Arguments:
- inputs: bfloat16 [1024, 2048], P('expert', 'dp'), may hold values from -6 to 6
- out_grad: bfloat16 [1024, 2048], P('expert', 'dp'), may hold values from -6 to 6
- gate_probs: float32 [1024, 2], P('expert'), may hold values from 0.1 to 1
- expert_ids: int32 [1024, 2], P('expert'), may hold values from 0 to 7, all different within a row; in each aligned block of 128 rows (0 to 127, 128 to 255, ...) at most 48 rows name the same one
- gate_proj: bfloat16 [8, 2048, 2304], P('expert', None, 'dp'), may hold values from -0.125 to 0.125
- down_proj: bfloat16 [8, 2304, 2048], P('expert', 'dp'), may hold values from -0.125 to 0.125
Outputs:
- layer_out: bfloat16 [1024, 2048], P('expert', 'dp')
- in_grad: bfloat16 [1024, 2048], P('expert', 'dp')
- prob_grad: float32 [1024, 2], P('expert')
The draws below stay inside these ranges and needn't reach their ends.
Inputs may be any that keep to these rules, and one draw needn't show every extreme that they name: `expert_ids`: each token names two different experts. Within each home group of 128 tokens no expert is named by more than 48 tokens, and in every draw some group names some expert exactly 48 times.
All inputs are finite; a program needn't handle non-finite values.
Results may differ from the reference program's by a relative error of at most 0.012.
Values may be sent and summed in bfloat16 or wider, within the bound.
A program may use at most 64 MiB of HBM per device.

```python
import math
import jax
import jax.numpy as jnp
import numpy as np
from jax import lax

D = 2048
HID_DEV = 576
TOK_DEV = 128
FF = 2304
EXPERTS = 8
CAP = 48
TOKENS = 1024


def shard_levels(own_key, extent, pieces, smallest, top_value):
    gain, own = 1.0, jax.random.fold_in(own_key, 6)
    for dim, shards_of in pieces:
        heights = jnp.exp(jax.random.uniform(jax.random.fold_in(own, dim), (shards_of,), jnp.float32, smallest / len(pieces), top_value / len(pieces)))
        gain = gain * jnp.repeat(heights, extent[dim] // shards_of).reshape([-1 if axis == dim else 1 for axis in range(len(extent))])
    return gain


def assign_block(stream_key, own, number, rows, count, top, reach, lean):
    ranking = jax.random.permutation(stream_key, count)
    heavy_load, ordinary = portions_of(count, rows * top, reach, lean, True), portions_of(count, rows * top, reach, lean, False)
    places = jnp.arange(count)

    def named(tallies, rotation):
        used = int((tallies > 0).sum())
        fixed = max(1, used // 4)
        passed = fixed + (places - fixed + rotation * (used - fixed)) % max(1, count - fixed)
        return jnp.zeros((count,), jnp.int32).at[ranking[jnp.where(places < fixed, places, passed)]].set(jnp.asarray(tallies, jnp.int32))

    tallies = jnp.where(number % 4 == 0, named(heavy_load, number // 4), named(ordinary, number - number // 4 - 1))
    mixed = jax.random.permutation(jax.random.fold_in(own, 3), count)
    donor, receiver = mixed[0:count // 2 * 2:2], mixed[1:count // 2 * 2:2]
    room = jnp.minimum(tallies[donor] - 1, reach - tallies[receiver]) // 2
    room = jnp.where((donor == ranking[0]) | (receiver == ranking[0]) | (tallies[receiver] == 0), 0, jnp.maximum(room, 0))
    passed = jax.random.randint(jax.random.fold_in(own, 4), (count // 2,), 0, 1 << 20) % (room + 1)
    tallies = tallies.at[donor].add(-passed).at[receiver].add(passed)
    items = jnp.searchsorted(jnp.cumsum(tallies), jnp.arange(rows * top), side="right").astype(jnp.int32)
    table = items.reshape(top, rows).T
    table = table[jax.random.permutation(jax.random.fold_in(own, 1), rows)]
    rotation = jax.random.randint(jax.random.fold_in(own, 2), (rows, 1), 0, top)
    return jnp.take_along_axis(table, (jnp.arange(top)[None, :] + rotation) % top, axis=1)


def portions_of(amount, total, limit, slope, full):
    loads = [(1 << 20) // math.isqrt(grade ** slope) + 1 for grade in range(1, amount + 1)]
    largest = limit if full else min(limit, max(-(-total // amount), total * loads[0] // sum(loads)))
    least = 1 if total - largest >= amount - 1 else 0
    counts, surplus = [largest] + [least] * (amount - 1), total - largest - least * (amount - 1)
    while surplus > 0:
        candidates = [i for i in range(1, amount) if counts[i] < largest] or [i for i in range(1, amount) if counts[i] < limit]
        whole, left = sum([loads[i] for i in candidates]), surplus
        for i in candidates:
            addition = min(limit - counts[i], max(1, left * loads[i] // whole), surplus)
            counts[i] = counts[i] + addition
            surplus = surplus - addition
    return np.array(counts)


def gaussian(own_key, dims, deviation, reach, cuts=(), kind=jnp.bfloat16):
    values = deviation * jax.random.normal(own_key, dims, jnp.float32)
    if cuts:
        values = values * shard_levels(own_key, dims, cuts, -0.22, 0.18)
    return jnp.clip(values, -reach, reach).astype(kind)


def setup_inputs(seed: int = 0) -> dict:
    key_list = jax.random.split(jax.random.key(seed), 7)
    inputs = gaussian(key_list[0], (TOKENS, D), 1.0, 6.0, ((0, 8), (1, 4)))
    out_grad = gaussian(key_list[1], (TOKENS, D), 1.0, 6.0, ((0, 8), (1, 4)))
    gate_probs = jnp.clip(0.1 + 0.9 * jax.random.uniform(key_list[2], (TOKENS, 2), jnp.float32) ** shard_levels(key_list[2], (TOKENS, 2), ((0, 8),), -0.2, 0.2), 0.1, 1.0)
    expert_ids_keys = jax.random.split(jax.random.fold_in(key_list[3], 1), TOKENS // TOK_DEV)
    expert_ids_turns = jax.random.permutation(jax.random.fold_in(key_list[3], 3), TOKENS // TOK_DEV)
    expert_ids = jax.vmap(lambda own, number: assign_block(jax.random.fold_in(key_list[3], 2), own, number, TOK_DEV, EXPERTS, 2, CAP, 2))(expert_ids_keys, expert_ids_turns).reshape((TOKENS, 2))
    gate_proj = gaussian(key_list[4], (EXPERTS, D, FF), D ** -0.5, 0.125, ((0, 8), (2, 4)))
    down_proj = gaussian(key_list[5], (EXPERTS, FF, D), FF ** -0.5, 0.125, ((0, 8), (1, 4)))
    return {"inputs": inputs, "out_grad": out_grad, "gate_probs": gate_probs, "expert_ids": expert_ids, "gate_proj": gate_proj, "down_proj": down_proj}


def block_sum(parts):
    rounded = lax.optimization_barrier(parts.astype(jnp.bfloat16))
    return jnp.sum(rounded.astype(jnp.float32), axis=0).astype(jnp.bfloat16)


def reference(inputs, out_grad, gate_probs, expert_ids, gate_proj, down_proj):
    homes = EXPERTS
    blocks = FF // HID_DEV
    copies = 2 * TOK_DEV
    flat = expert_ids.reshape(homes, copies)
    onehot = (flat[:, :, None] == jnp.arange(EXPERTS, dtype=jnp.int32)[None, None, :]).astype(jnp.int32)
    before = jnp.cumsum(onehot, axis=1) - onehot
    position = jnp.sum(before * onehot, axis=2).astype(jnp.int32)
    home = jnp.broadcast_to(jnp.arange(homes, dtype=jnp.int32)[:, None], (homes, copies))
    copy_id = home * copies + jnp.arange(copies, dtype=jnp.int32)[None, :]
    table = jnp.full((EXPERTS, homes, CAP), 2 * TOKENS, jnp.int32).at[flat, home, position].set(copy_id)
    table = table.reshape(EXPERTS, homes * CAP)
    x_pad = jnp.concatenate([inputs, jnp.zeros((1, D), jnp.bfloat16)], axis=0)
    dy_pad = jnp.concatenate([out_grad, jnp.zeros((1, D), jnp.bfloat16)], axis=0)
    p_pad = jnp.concatenate([gate_probs.reshape(-1), jnp.zeros((1,), jnp.float32)])

    def one_expert(pack):
        w_gate, w_down, slots = pack
        token = jnp.where(slots < 2 * TOKENS, slots // 2, TOKENS).astype(jnp.int32)
        x_rows = x_pad[token]
        prob = p_pad[slots][:, None]
        pre_gate = jnp.dot(x_rows, w_gate, preferred_element_type=jnp.float32)
        sig = jax.nn.sigmoid(pre_gate)
        hidden = (pre_gate * sig).astype(jnp.bfloat16)
        rows = hidden.shape[0]
        out_parts = jnp.einsum('rnh,nhd->nrd', hidden.reshape(rows, blocks, HID_DEV).astype(jnp.float32),
                               w_down.reshape(blocks, HID_DEV, D).astype(jnp.float32))
        expert_out = block_sum(out_parts)
        slot_grad = (prob * dy_pad[token].astype(jnp.float32)).astype(jnp.bfloat16)
        back = lax.dot_general(slot_grad, w_down, (((1,), (1,)), ((), ())), preferred_element_type=jnp.float32)
        gate_term = (back * sig * (1.0 + pre_gate * (1.0 - sig))).astype(jnp.bfloat16)
        in_parts = jnp.einsum('rnh,dnh->nrd', gate_term.reshape(rows, blocks, HID_DEV).astype(jnp.float32),
                              w_gate.reshape(D, blocks, HID_DEV).astype(jnp.float32))
        copy_grad = block_sum(in_parts)
        return expert_out, copy_grad

    expert_out, copy_grad = lax.map(one_expert, (gate_proj, down_proj, table))
    where = home * CAP + position
    out_copy = expert_out[flat, where].reshape(TOKENS, 2, D).astype(jnp.float32)
    grad_copy = copy_grad[flat, where].reshape(TOKENS, 2, D).astype(jnp.float32)
    layer_out = jnp.sum(gate_probs[:, :, None] * out_copy, axis=1).astype(jnp.bfloat16)
    in_grad = jnp.sum(grad_copy, axis=1).astype(jnp.bfloat16)
    prob_grad = jnp.sum(out_grad.astype(jnp.float32)[:, None, :] * out_copy, axis=2)
    return layer_out, in_grad, prob_grad
```

```python
import functools

import jax
import jax.numpy as jnp
from jax import lax
from jax.experimental import pallas as pl
from jax.experimental.pallas import tpu as pltpu
from jax.sharding import PartitionSpec as P

MESH = pl.DeviceIdType.MESH
LANES = 128


def flip(a, b, size):
    out, bit = 0, 1
    while bit < size:
        out = out + ((a // bit + b // bit) % 2) * bit
        bit *= 2
    return out


def nt_dot(left, right):
    return lax.dot_general(
        left, right, (((1,), (1,)), ((), ())), preferred_element_type=jnp.float32
    )


def nn_dot(left, right):
    return jnp.dot(left, right, preferred_element_type=jnp.float32)


def moe_kernel(
    parts, experts, cap,
    x_ref, dy_ref, p_ref, id_ref, wg_hbm, wd_hbm,
    both_ref, pg_ref,
    wg, wd, home, pick0, pick1, spread, weight,
    send, recv, pre, back, hid, gterm, rsend, rrecv,
    part, gathered, joined, own, pacc, psend, precv, fsum, nsum, fsend,
    w_sem, ag_send, ag_recv, loc_sem, a_send, a_recv, far_recv, next_recv,
    rloc_sem, r_send, r_recv, rfar_recv, rnext_recv, f_send, rf_send,
    s_send, s_recv, j_recv, p_send, p_recv, h_recv, n_recv,
):
    z = lax.axis_index("dp")
    me = lax.axis_index("expert")
    far = flip(me, experts - 2, experts)
    far2 = flip(me, experts - 1, experts)
    tokens, cols = x_ref.shape
    rows = experts * cap
    bf16, f32 = jnp.bfloat16, jnp.float32
    rightward, leftward = z + 1 < parts, z > 0

    load_g = pltpu.make_async_copy(wg_hbm.at[0], wg, w_sem.at[0])
    load_d = pltpu.make_async_copy(wd_hbm.at[0], wd, w_sem.at[1])
    load_g.start()
    load_d.start()

    barrier = pltpu.get_barrier_semaphore()

    @pl.loop(1, parts)
    def _(i):
        pl.semaphore_signal(
            barrier, inc=1, device_id={"dp": flip(z, i, parts)}, device_id_type=MESH
        )

    @pl.loop(1, experts)
    def _(j):
        pl.semaphore_signal(
            barrier, inc=1, device_id={"expert": flip(me, j, experts)}, device_id_type=MESH
        )

    lowhalf = 2 * z < parts
    paired = 2 * jnp.where(lowhalf, z, parts - 1 - z)

    def nearest(n):
        near_by = z + (n + 1) // 2 * (1 - 2 * (n % 2))
        beyond = jnp.where(lowhalf, n, parts - 1 - n)
        return jnp.where(n <= paired, near_by, beyond)

    def adjacent(chunk):
        return (chunk - z) * (chunk - z) == 1

    across = lax.broadcasted_iota(jnp.int32, (tokens, tokens), 1)
    down = lax.broadcasted_iota(jnp.int32, (tokens, tokens), 0)

    def column(row):
        return jnp.sum(jnp.where(across == down, row, 0), axis=1, keepdims=True)

    id0, id1 = column(id_ref[0:1, :]), column(id_ref[1:2, :])
    p0, p1 = column(p_ref[0:1, :]), column(p_ref[1:2, :])
    lane = lax.broadcasted_iota(jnp.int32, (tokens, LANES), 1)
    hot0 = (lane == id0).astype(f32)
    hot1 = (lane == id1).astype(f32)
    earlier = (across < down).astype(f32)
    count = nn_dot(earlier.astype(bf16), (hot0 + hot1).astype(bf16))
    pos0 = jnp.sum(count * hot0, axis=1, keepdims=True)
    pos1 = jnp.sum(count * hot1, axis=1, keepdims=True)
    slot = lax.broadcasted_iota(jnp.int32, (tokens, rows), 1)
    t0 = (slot == id0 * cap + pos0.astype(jnp.int32)).astype(f32)
    t1 = (slot == id1 * cap + pos1.astype(jnp.int32)).astype(f32)
    pick0[...] = t0.astype(bf16)
    pick1[...] = t1.astype(bf16)
    spread[...] = jnp.transpose(t0 + t1).astype(bf16)
    weight[...] = jnp.sum(jnp.transpose(t0 * p0 + t1 * p1), axis=1, keepdims=True)

    home[z, 0] = x_ref[...]
    home[z, 1] = dy_ref[...]
    pre[...] = jnp.zeros_like(pre)
    back[...] = jnp.zeros_like(back)
    pacc[...] = jnp.zeros_like(pacc)

    @pl.loop(1, parts)
    def _(n):
        chunk = nearest(n)
        rrecv[0, chunk, far] = jnp.zeros((cap, cols), bf16)
        rrecv[1, chunk, far] = jnp.zeros((cap, cols), bf16)

        @pl.when(adjacent(chunk))
        def _():
            rrecv[0, chunk, far2] = jnp.zeros((cap, cols), bf16)
            rrecv[1, chunk, far2] = jnp.zeros((cap, cols), bf16)

    with jax.named_scope("entry"):
        pl.semaphore_wait(barrier, parts - 1 + experts - 1)

    def pass_on(kind, chunk, neighbour):
        pltpu.make_async_remote_copy(
            src_ref=home.at[chunk, kind], dst_ref=home.at[chunk, kind],
            send_sem=ag_send, recv_sem=ag_recv.at[kind, chunk],
            device_id={"dp": neighbour}, device_id_type=MESH,
        ).start()

    @pl.when(rightward)
    def _():
        pass_on(0, z, z + 1)
        pass_on(1, z, z + 1)

    @pl.when(leftward)
    def _():
        pass_on(0, z, z - 1)
        pass_on(1, z, z - 1)

    def to_peer(source, target, kind, chunk, peer, send_sem, recv_sem):
        pltpu.make_async_remote_copy(
            src_ref=source.at[kind, chunk, peer], dst_ref=target.at[kind, chunk, me],
            send_sem=send_sem, recv_sem=recv_sem.at[kind, chunk],
            device_id={"expert": peer}, device_id_type=MESH,
        ).start()

    def exchange(source, target, kind, chunk, send_sem, recv_sem, local_sem):
        @pl.loop(3, experts)
        def _(j):
            to_peer(
                source, target, kind, chunk, flip(me, experts - j, experts), send_sem, recv_sem
            )

        pltpu.make_async_copy(
            source.at[kind, chunk, me], target.at[kind, chunk, me], local_sem.at[kind, chunk]
        ).start()

    def exchanged(source, target, kind, chunk, recv_sem, local_sem):
        pltpu.make_async_copy(
            source.at[kind, chunk, me], target.at[kind, chunk, me], local_sem.at[kind, chunk]
        ).wait()
        several = target.at[kind, chunk, pl.ds(0, experts - 3)]
        pltpu.make_async_copy(several, several, recv_sem.at[kind, chunk]).wait()

    def arrived(block, sem):
        pltpu.make_async_copy(block, block, sem).wait()

    def slot_rows(kind, chunk):
        picked = nn_dot(spread[...], home[chunk, kind])
        if kind == 1:
            picked = weight[...] * picked
        send[kind, chunk] = picked.astype(bf16).reshape(experts, cap, cols)

    def dispatch_own(kind):
        slot_rows(kind, z)
        to_peer(send, recv, kind, z, far, f_send, far_recv)
        to_peer(send, recv, kind, z, far2, f_send, next_recv)
        exchange(send, recv, kind, z, a_send, a_recv, loc_sem)

    def dispatch(kind, chunk):
        arrived(home.at[chunk, kind], ag_recv.at[kind, chunk])

        @pl.when((chunk < z) & rightward)
        def _():
            pass_on(kind, chunk, z + 1)

        @pl.when((chunk > z) & leftward)
        def _():
            pass_on(kind, chunk, z - 1)

        slot_rows(kind, chunk)

        @pl.when(jnp.logical_not(adjacent(chunk)))
        def _():
            to_peer(send, recv, kind, chunk, far2, f_send, next_recv)

        exchange(send, recv, kind, chunk, a_send, a_recv, loc_sem)

    def relay():
        for kind in (0, 1):
            arrived(recv.at[kind, z, far], far_recv.at[kind, z])
            arrived(recv.at[kind, z, far2], next_recv.at[kind, z])

        def onward(kind, peer, sem, chunk):
            pltpu.make_async_remote_copy(
                src_ref=recv.at[kind, z, peer], dst_ref=recv.at[kind, z, peer],
                send_sem=f_send, recv_sem=sem.at[kind, z],
                device_id={"dp": chunk}, device_id_type=MESH,
            ).start()

        @pl.loop(1, parts)
        def _(n):
            for kind in (0, 1):
                onward(kind, far, far_recv, nearest(parts - n))

        for kind in (0, 1):

            @pl.when(rightward)
            def _():
                onward(kind, far2, next_recv, z + 1)

            @pl.when(leftward)
            def _():
                onward(kind, far2, next_recv, z - 1)

    inner = rightward & leftward
    dispatch_own(0)
    dispatch_own(1)
    dispatch(0, nearest(1))
    dispatch(1, nearest(1))

    @pl.when(jnp.logical_not(inner))
    def _():
        relay()

    @pl.loop(2, parts)
    def _(n):
        dispatch(0, nearest(n))
        dispatch(1, nearest(n))

    @pl.when(inner)
    def _():
        relay()

    def contract(kind, total, w, chunk):
        start = pl.multiple_of(chunk * cols, cols)
        exchanged(send, recv, kind, chunk, a_recv, loc_sem)

        @pl.when(chunk != z)
        def _():
            arrived(recv.at[kind, chunk, far], far_recv.at[kind, chunk])
            arrived(recv.at[kind, chunk, far2], next_recv.at[kind, chunk])

        total[...] += nt_dot(recv[kind, chunk].reshape(rows, cols), w[:, pl.ds(start, cols)])

    def produce(kind, term, w, chunk):
        start = pl.multiple_of(chunk * cols, cols)
        rsend[kind, chunk] = (
            nn_dot(term[...], w[:, pl.ds(start, cols)]).astype(bf16).reshape(experts, cap, cols)
        )

    def give_back(kind, term, w, chunk):
        produce(kind, term, w, chunk)
        pltpu.make_async_remote_copy(
            src_ref=rsend.at[kind, chunk, far], dst_ref=fsum.at[kind, z],
            send_sem=rf_send, recv_sem=h_recv.at[kind],
            device_id={"dp": chunk}, device_id_type=MESH,
        ).start()

        def to_next(side):
            pltpu.make_async_remote_copy(
                src_ref=rsend.at[kind, chunk, far2], dst_ref=nsum.at[kind, side],
                send_sem=rf_send, recv_sem=n_recv.at[kind, side],
                device_id={"dp": chunk}, device_id_type=MESH,
            ).start()

        @pl.when(chunk == z + 1)
        def _():
            to_next(0)

        @pl.when(chunk == z - 1)
        def _():
            to_next(1)

        @pl.when(jnp.logical_not(adjacent(chunk)))
        def _():
            to_peer(rsend, rrecv, kind, chunk, far2, rf_send, rnext_recv)

        exchange(rsend, rrecv, kind, chunk, r_send, r_recv, rloc_sem)

    def give_own(kind, term, w):
        produce(kind, term, w, z)
        exchange(rsend, rrecv, kind, z, r_send, r_recv, rloc_sem)

    def give_sums(kind):
        sums = fsum.at[kind, pl.ds(0, parts - 1)]
        pltpu.make_async_copy(sums, sums, h_recv.at[kind]).wait()
        fsend[kind, 0] = lax.fori_loop(
            1, parts, lambda i, total: total + fsum[kind, flip(z, i, parts)].astype(f32),
            rsend[kind, z, far].astype(f32),
        ).astype(bf16)
        pltpu.make_async_remote_copy(
            src_ref=fsend.at[kind, 0], dst_ref=rrecv.at[kind, z, me],
            send_sem=rf_send, recv_sem=rfar_recv.at[kind],
            device_id={"expert": far}, device_id_type=MESH,
        ).start()

        @pl.when(leftward)
        def _():
            arrived(nsum.at[kind, 0], n_recv.at[kind, 0])

        @pl.when(rightward)
        def _():
            arrived(nsum.at[kind, 1], n_recv.at[kind, 1])

        fsend[kind, 1] = (
            rsend[kind, z, far2].astype(f32)
            + jnp.where(leftward, nsum[kind, 0].astype(f32), 0.0)
            + jnp.where(rightward, nsum[kind, 1].astype(f32), 0.0)
        ).astype(bf16)
        pltpu.make_async_remote_copy(
            src_ref=fsend.at[kind, 1], dst_ref=rrecv.at[kind, z, me],
            send_sem=rf_send, recv_sem=rnext_recv.at[kind, z],
            device_id={"expert": far2}, device_id_type=MESH,
        ).start()

    def combine(kind, chunk):
        exchanged(rsend, rrecv, kind, chunk, r_recv, rloc_sem)

        @pl.when(jnp.logical_not(adjacent(chunk)))
        def _():
            arrived(rrecv.at[kind, chunk, far2], rnext_recv.at[kind, chunk])

        block = rrecv[kind, chunk].reshape(rows, cols)
        if kind == 1:
            own[1] = nn_dot(pick0[...] + pick1[...], block)
            return
        out0, out1 = nn_dot(pick0[...], block), nn_dot(pick1[...], block)
        dy = home[chunk, 1].astype(f32)
        s0 = jnp.sum(dy * out0, axis=1, keepdims=True)
        s1 = jnp.sum(dy * out1, axis=1, keepdims=True)
        pacc[...] += jnp.where(lane == 0, s0, 0.0) + jnp.where(lane == 1, s1, 0.0)
        own[0] = p0 * out0 + p1 * out1

    def add_in(kind, sum_in, sem):
        pltpu.make_async_copy(sum_in, sum_in, sem).wait()
        own[kind] += sum_in[...].astype(f32)

    def sum_on(kind, chunk):
        combine(kind, chunk)
        upward = chunk > z
        apart = jnp.where(upward, chunk - z, z - chunk)
        stops = (apart % 2 == 1) & (apart > 1)

        @pl.when((apart % 2 == 0) & jnp.where(upward, leftward, rightward))
        def _():
            add_in(kind, joined.at[kind, chunk], j_recv.at[kind, chunk])

        part[kind, chunk] = own[kind].astype(bf16)

        @pl.when(stops)
        def _():
            pltpu.make_async_remote_copy(
                src_ref=part.at[kind, chunk], dst_ref=joined.at[kind, chunk],
                send_sem=s_send, recv_sem=j_recv.at[kind, chunk],
                device_id={"dp": jnp.where(upward, z + 1, z - 1)}, device_id_type=MESH,
            ).start()

        @pl.when(jnp.logical_not(stops))
        def _():
            pltpu.make_async_remote_copy(
                src_ref=part.at[kind, chunk], dst_ref=gathered.at[kind, z],
                send_sem=s_send, recv_sem=s_recv.at[kind, z],
                device_id={"dp": chunk}, device_id_type=MESH,
            ).start()

    def sum_own(kind):
        arrived(rrecv.at[kind, z, far], rfar_recv.at[kind])
        combine(kind, z)

        @pl.loop(1, parts)
        def _(n):
            source = nearest(parts - n)
            apart = jnp.where(source > z, source - z, z - source)

            @pl.when((apart % 2 == 0) | (apart == 1))
            def _():
                add_in(kind, gathered.at[kind, source], s_recv.at[kind, source])

        both_ref[kind] = own[kind].astype(bf16)

    load_g.wait()

    @pl.loop(0, parts)
    def _(n):
        contract(0, pre, wg, nearest(n))

    hid[...] = (pre[...] * jax.nn.sigmoid(pre[...])).astype(bf16)
    load_d.wait()
    split = parts // 2 + 1

    @pl.loop(1, split)
    def _(n):
        give_back(0, hid, wd, nearest(parts - n))

    @pl.loop(0, parts)
    def _(n):
        contract(1, back, wd, nearest(n))

    v = pre[...]
    sig = jax.nn.sigmoid(v)
    gterm[...] = (back[...] * sig * (1.0 + v * (1.0 - sig))).astype(bf16)

    @pl.loop(1, split)
    def _(n):
        give_back(1, gterm, wg, nearest(parts - n))

    @pl.loop(split, parts)
    def _(n):
        give_back(0, hid, wd, nearest(parts - n))
        give_back(1, gterm, wg, nearest(parts - n))

    give_own(0, hid, wd)
    give_own(1, gterm, wg)

    @pl.loop(1, split)
    def _(n):
        sum_on(0, nearest(parts - n))

    give_sums(0)

    @pl.loop(1, split)
    def _(n):
        sum_on(1, nearest(parts - n))

    give_sums(1)

    @pl.loop(split, parts)
    def _(n):
        sum_on(0, nearest(parts - n))
        sum_on(1, nearest(parts - n))

    sum_own(0)
    psend[...] = jnp.transpose(pacc[...])[0:8]

    @pl.loop(1, parts)
    def _(i):
        pltpu.make_async_remote_copy(
            src_ref=psend, dst_ref=precv.at[z],
            send_sem=p_send, recv_sem=p_recv,
            device_id={"dp": flip(z, i, parts)}, device_id_type=MESH,
        ).start()

    sum_own(1)

    rest = precv.at[pl.ds(0, parts - 1)]
    with jax.named_scope("prob_wait"):
        pltpu.make_async_copy(rest, rest, p_recv).wait()
    pg_ref[...] = psend[0:2]

    @pl.loop(1, parts)
    def _(i):
        pg_ref[...] += precv[flip(z, i, parts), 0:2]

    passed = home.at[z]

    @pl.when(rightward)
    def _():
        @pl.loop(0, z + 1)
        def _(i):
            pltpu.make_async_copy(passed, passed, ag_send).wait()

    @pl.when(leftward)
    def _():
        @pl.loop(0, parts - z)
        def _(i):
            pltpu.make_async_copy(passed, passed, ag_send).wait()

    pltpu.make_async_copy(rest, rest, p_send).wait()
    several = send.at[0, 0, pl.ds(0, experts - 3)]
    others = part.at[0, pl.ds(0, parts - 1)]
    row = fsum.at[0]

    @pl.loop(0, 2)
    def _(kind):
        pltpu.make_async_copy(others, others, s_send).wait()

        @pl.loop(0, parts)
        def _(i):
            pltpu.make_async_copy(several, several, a_send).wait()
            pltpu.make_async_copy(several, several, r_send).wait()

        @pl.loop(0, 2)
        def _(i):
            pltpu.make_async_copy(row, row, f_send).wait()
            pltpu.make_async_copy(row, row, rf_send).wait()


def split_kernel(both_ref, prob_ref, lo_ref, ig_ref, pg_ref):
    lo_ref[...] = both_ref[0]
    ig_ref[...] = both_ref[1]
    pg_ref[...] = prob_ref[...]


def per_device(inputs, out_grad, gate_probs, expert_ids, gate_proj, down_proj):
    parts = lax.axis_size("dp")
    experts = lax.axis_size("expert")
    tokens, cols = inputs.shape
    cap = -(-(3 * tokens // experts) // 16) * 16
    rows = experts * cap
    _, width, hidden = gate_proj.shape
    bf16, f32 = jnp.bfloat16, jnp.float32
    vmem = pl.BlockSpec(memory_space=pltpu.VMEM)
    hbm = pl.BlockSpec(memory_space=pl.ANY)
    dma = pltpu.SemaphoreType.DMA
    both, prob = pl.pallas_call(
        functools.partial(moe_kernel, parts, experts, cap),
        out_shape=(
            jax.ShapeDtypeStruct((2, tokens, cols), bf16),
            jax.ShapeDtypeStruct((2, tokens), f32),
        ),
        in_specs=[vmem, vmem, vmem, vmem, hbm, hbm],
        out_specs=(vmem, vmem),
        scratch_shapes=[
            pltpu.VMEM((hidden, width), bf16),
            pltpu.VMEM((hidden, width), bf16),
            pltpu.VMEM((parts, 2, tokens, cols), bf16),
            pltpu.VMEM((tokens, rows), bf16),
            pltpu.VMEM((tokens, rows), bf16),
            pltpu.VMEM((rows, tokens), bf16),
            pltpu.VMEM((rows, 1), f32),
            pltpu.VMEM((2, parts, experts, cap, cols), bf16),
            pltpu.VMEM((2, parts, experts, cap, cols), bf16),
            pltpu.VMEM((rows, hidden), f32),
            pltpu.VMEM((rows, hidden), f32),
            pltpu.VMEM((rows, hidden), bf16),
            pltpu.VMEM((rows, hidden), bf16),
            pltpu.VMEM((2, parts, experts, cap, cols), bf16),
            pltpu.VMEM((2, parts, experts, cap, cols), bf16),
            pltpu.VMEM((2, parts, tokens, cols), bf16),
            pltpu.VMEM((2, parts, tokens, cols), bf16),
            pltpu.VMEM((2, parts, tokens, cols), bf16),
            pltpu.VMEM((2, tokens, cols), f32),
            pltpu.VMEM((tokens, LANES), f32),
            pltpu.VMEM((8, tokens), f32),
            pltpu.VMEM((parts, 8, tokens), f32),
            pltpu.VMEM((2, parts, cap, cols), bf16),
            pltpu.VMEM((2, 2, cap, cols), bf16),
            pltpu.VMEM((2, 2, cap, cols), bf16),
            dma((2,)), dma, dma((2, parts)), dma((2, parts)), dma, dma((2, parts)),
            dma((2, parts)), dma((2, parts)),
            dma((2, parts)), dma, dma((2, parts)), dma((2,)), dma((2, parts)), dma, dma,
            dma, dma((2, parts)), dma((2, parts)), dma, dma, dma((2,)), dma((2, 2)),
        ],
        compiler_params=pltpu.CompilerParams(
            collective_id=0, has_side_effects=True, vmem_limit_bytes=56 * 1024 * 1024
        ),
    )(inputs, out_grad, gate_probs.T, expert_ids.T, jnp.swapaxes(gate_proj, 1, 2), down_proj)
    layer_out, in_grad, prob_grad = pl.pallas_call(
        split_kernel,
        out_shape=(
            jax.ShapeDtypeStruct((tokens, cols), bf16),
            jax.ShapeDtypeStruct((tokens, cols), bf16),
            jax.ShapeDtypeStruct((2, tokens), f32),
        ),
        in_specs=[vmem, vmem],
        out_specs=(vmem, vmem, vmem),
    )(both, prob)
    return layer_out, in_grad, prob_grad.T


def solution(mesh):
    placed = (
        P("expert", "dp"),
        P("expert", "dp"),
        P("expert", None),
        P("expert", None),
        P("expert", None, "dp"),
        P("expert", "dp", None),
    )
    return jax.shard_map(
        per_device,
        mesh=mesh,
        in_specs=placed,
        out_specs=(P("expert", "dp"), P("expert", "dp"), P("expert", None)),
        check_vma=False,
    )
```

```python
import functools

import jax
import jax.numpy as jnp
from jax import lax
from jax.experimental import pallas as pl
from jax.experimental.pallas import tpu as pltpu
from jax.sharding import PartitionSpec as P

MESH = pl.DeviceIdType.MESH
LANES = 128


def flip(a, b, size):
    out, bit = 0, 1
    while bit < size:
        out = out + ((a // bit + b // bit) % 2) * bit
        bit *= 2
    return out


def nt_dot(left, right):
    return lax.dot_general(
        left, right, (((1,), (1,)), ((), ())), preferred_element_type=jnp.float32
    )


def nn_dot(left, right):
    return jnp.dot(left, right, preferred_element_type=jnp.float32)


def moe_kernel(
    parts, experts, cap,
    x_ref, dy_ref, p_ref, id_ref, wg_hbm, wd_hbm,
    both_ref, pg_ref,
    wg, wd, home, pick0, pick1, spread, weight,
    send, recv, pre, back, hid, gterm, rsend, rrecv,
    part, gathered, joined, own, pacc, psend, precv, fsum, nsum, fsend,
    w_sem, ag_send, ag_recv, loc_sem, a_send, a_recv, far_recv, next_recv,
    rloc_sem, r_send, r_recv, rfar_recv, rnext_recv, f_send, rf_send,
    s_send, s_recv, j_recv, p_send, p_recv, h_recv, n_recv,
):
    z = lax.axis_index("dp")
    me = lax.axis_index("expert")
    far = flip(me, experts - 2, experts)
    far2 = flip(me, experts - 1, experts)
    tokens, cols = x_ref.shape
    rows = experts * cap
    bf16, f32 = jnp.bfloat16, jnp.float32
    rightward, leftward = z + 1 < parts, z > 0

    load_g = pltpu.make_async_copy(wg_hbm.at[0], wg, w_sem.at[0])
    load_d = pltpu.make_async_copy(wd_hbm.at[0], wd, w_sem.at[1])
    load_g.start()
    load_d.start()

    barrier = pltpu.get_barrier_semaphore()

    @pl.loop(1, parts)
    def _(i):
        pl.semaphore_signal(
            barrier, inc=1, device_id={"dp": flip(z, i, parts)}, device_id_type=MESH
        )

    @pl.loop(1, experts)
    def _(j):
        pl.semaphore_signal(
            barrier, inc=1, device_id={"expert": flip(me, j, experts)}, device_id_type=MESH
        )

    lowhalf = 2 * z < parts
    paired = 2 * jnp.where(lowhalf, z, parts - 1 - z)

    def nearest(n):
        near_by = z + (n + 1) // 2 * (1 - 2 * (n % 2))
        beyond = jnp.where(lowhalf, n, parts - 1 - n)
        return jnp.where(n <= paired, near_by, beyond)

    def adjacent(chunk):
        return (chunk - z) * (chunk - z) == 1

    across = lax.broadcasted_iota(jnp.int32, (tokens, tokens), 1)
    down = lax.broadcasted_iota(jnp.int32, (tokens, tokens), 0)

    def column(row):
        return jnp.sum(jnp.where(across == down, row, 0), axis=1, keepdims=True)

    id0, id1 = column(id_ref[0:1, :]), column(id_ref[1:2, :])
    p0, p1 = column(p_ref[0:1, :]), column(p_ref[1:2, :])
    lane = lax.broadcasted_iota(jnp.int32, (tokens, LANES), 1)
    hot0 = (lane == id0).astype(f32)
    hot1 = (lane == id1).astype(f32)
    earlier = (across < down).astype(f32)
    count = nn_dot(earlier.astype(bf16), (hot0 + hot1).astype(bf16))
    pos0 = jnp.sum(count * hot0, axis=1, keepdims=True)
    pos1 = jnp.sum(count * hot1, axis=1, keepdims=True)
    slot = lax.broadcasted_iota(jnp.int32, (tokens, rows), 1)
    t0 = (slot == id0 * cap + pos0.astype(jnp.int32)).astype(f32)
    t1 = (slot == id1 * cap + pos1.astype(jnp.int32)).astype(f32)
    pick0[...] = t0.astype(bf16)
    pick1[...] = t1.astype(bf16)
    spread[...] = jnp.transpose(t0 + t1).astype(bf16)
    weight[...] = jnp.sum(jnp.transpose(t0 * p0 + t1 * p1), axis=1, keepdims=True)

    home[z, 0] = x_ref[...]
    home[z, 1] = dy_ref[...]
    with jax.named_scope("entry"):
        pl.semaphore_wait(barrier, parts - 1 + experts - 1)

    def pass_on(kind, chunk, neighbour):
        pltpu.make_async_remote_copy(
            src_ref=home.at[chunk, kind], dst_ref=home.at[chunk, kind],
            send_sem=ag_send, recv_sem=ag_recv.at[kind, chunk],
            device_id={"dp": neighbour}, device_id_type=MESH,
        ).start()

    @pl.when(rightward)
    def _():
        pass_on(0, z, z + 1)
        pass_on(1, z, z + 1)

    @pl.when(leftward)
    def _():
        pass_on(0, z, z - 1)
        pass_on(1, z, z - 1)

    def to_peer(source, target, kind, chunk, peer, send_sem, recv_sem):
        pltpu.make_async_remote_copy(
            src_ref=source.at[kind, chunk, peer], dst_ref=target.at[kind, chunk, me],
            send_sem=send_sem, recv_sem=recv_sem.at[kind, chunk],
            device_id={"expert": peer}, device_id_type=MESH,
        ).start()

    def exchange(source, target, kind, chunk, send_sem, recv_sem, local_sem):
        @pl.loop(3, experts)
        def _(j):
            to_peer(
                source, target, kind, chunk, flip(me, experts - j, experts), send_sem, recv_sem
            )

        pltpu.make_async_copy(
            source.at[kind, chunk, me], target.at[kind, chunk, me], local_sem.at[kind, chunk]
        ).start()

    def exchanged(source, target, kind, chunk, recv_sem, local_sem):
        pltpu.make_async_copy(
            source.at[kind, chunk, me], target.at[kind, chunk, me], local_sem.at[kind, chunk]
        ).wait()
        several = target.at[kind, chunk, pl.ds(0, experts - 3)]
        pltpu.make_async_copy(several, several, recv_sem.at[kind, chunk]).wait()

    def arrived(block, sem):
        pltpu.make_async_copy(block, block, sem).wait()

    def slot_rows(kind, chunk):
        picked = nn_dot(spread[...], home[chunk, kind])
        if kind == 1:
            picked = weight[...] * picked
        send[kind, chunk] = picked.astype(bf16).reshape(experts, cap, cols)

    def dispatch_own(kind):
        slot_rows(kind, z)
        to_peer(send, recv, kind, z, far, f_send, far_recv)
        to_peer(send, recv, kind, z, far2, f_send, next_recv)
        exchange(send, recv, kind, z, a_send, a_recv, loc_sem)

    def receive(kind, chunk):
        arrived(home.at[chunk, kind], ag_recv.at[kind, chunk])

        @pl.when((chunk < z) & rightward)
        def _():
            pass_on(kind, chunk, z + 1)

        @pl.when((chunk > z) & leftward)
        def _():
            pass_on(kind, chunk, z - 1)

    def dispatch(kind, chunk):
        slot_rows(kind, chunk)

        @pl.when(jnp.logical_not(adjacent(chunk)))
        def _():
            to_peer(send, recv, kind, chunk, far2, f_send, next_recv)

        exchange(send, recv, kind, chunk, a_send, a_recv, loc_sem)

    def relay():
        for kind in (0, 1):
            arrived(recv.at[kind, z, far], far_recv.at[kind, z])
            arrived(recv.at[kind, z, far2], next_recv.at[kind, z])

        def onward(kind, peer, sem, chunk):
            pltpu.make_async_remote_copy(
                src_ref=recv.at[kind, z, peer], dst_ref=recv.at[kind, z, peer],
                send_sem=f_send, recv_sem=sem.at[kind, z],
                device_id={"dp": chunk}, device_id_type=MESH,
            ).start()

        @pl.loop(1, parts)
        def _(n):
            for kind in (0, 1):
                onward(kind, far, far_recv, nearest(parts - n))

        for kind in (0, 1):

            @pl.when(rightward)
            def _():
                onward(kind, far2, next_recv, z + 1)

            @pl.when(leftward)
            def _():
                onward(kind, far2, next_recv, z - 1)

    inner = rightward & leftward
    dispatch_own(0)
    dispatch_own(1)
    pre[...] = jnp.zeros_like(pre)
    back[...] = jnp.zeros_like(back)
    pacc[...] = jnp.zeros_like(pacc)

    @pl.loop(1, parts)
    def _(n):
        chunk = nearest(n)
        rrecv[0, chunk, far] = jnp.zeros((cap, cols), bf16)
        rrecv[1, chunk, far] = jnp.zeros((cap, cols), bf16)

        @pl.when(adjacent(chunk))
        def _():
            rrecv[0, chunk, far2] = jnp.zeros((cap, cols), bf16)
            rrecv[1, chunk, far2] = jnp.zeros((cap, cols), bf16)

    @pl.loop(1, parts)
    def _(i):
        lower, upper = z - i, z + i
        for kind in (0, 1):
            for step in (receive, dispatch):

                @pl.when(lower >= 0)
                def _():
                    step(kind, lower)

                @pl.when(upper < parts)
                def _():
                    step(kind, upper)

        @pl.when((i == 1) & jnp.logical_not(inner))
        def _():
            relay()

    @pl.when(inner)
    def _():
        relay()

    def contract(kind, total, w, chunk):
        start = pl.multiple_of(chunk * cols, cols)
        exchanged(send, recv, kind, chunk, a_recv, loc_sem)

        @pl.when(chunk != z)
        def _():
            arrived(recv.at[kind, chunk, far], far_recv.at[kind, chunk])
            arrived(recv.at[kind, chunk, far2], next_recv.at[kind, chunk])

        total[...] += nt_dot(recv[kind, chunk].reshape(rows, cols), w[:, pl.ds(start, cols)])

    def produce(kind, term, w, chunk):
        start = pl.multiple_of(chunk * cols, cols)
        rsend[kind, chunk] = (
            nn_dot(term[...], w[:, pl.ds(start, cols)]).astype(bf16).reshape(experts, cap, cols)
        )

    def give_back(kind, term, w, chunk):
        produce(kind, term, w, chunk)
        pltpu.make_async_remote_copy(
            src_ref=rsend.at[kind, chunk, far], dst_ref=fsum.at[kind, z],
            send_sem=rf_send, recv_sem=h_recv.at[kind],
            device_id={"dp": chunk}, device_id_type=MESH,
        ).start()

        def to_next(side):
            pltpu.make_async_remote_copy(
                src_ref=rsend.at[kind, chunk, far2], dst_ref=nsum.at[kind, side],
                send_sem=rf_send, recv_sem=n_recv.at[kind, side],
                device_id={"dp": chunk}, device_id_type=MESH,
            ).start()

        @pl.when(chunk == z + 1)
        def _():
            to_next(0)

        @pl.when(chunk == z - 1)
        def _():
            to_next(1)

        @pl.when(jnp.logical_not(adjacent(chunk)))
        def _():
            to_peer(rsend, rrecv, kind, chunk, far2, rf_send, rnext_recv)

        exchange(rsend, rrecv, kind, chunk, r_send, r_recv, rloc_sem)

    def give_own(kind, term, w):
        produce(kind, term, w, z)
        exchange(rsend, rrecv, kind, z, r_send, r_recv, rloc_sem)

    def give_sums(kind):
        sums = fsum.at[kind, pl.ds(0, parts - 1)]
        pltpu.make_async_copy(sums, sums, h_recv.at[kind]).wait()
        fsend[kind, 0] = lax.fori_loop(
            1, parts, lambda i, total: total + fsum[kind, flip(z, i, parts)].astype(f32),
            rsend[kind, z, far].astype(f32),
        ).astype(bf16)
        pltpu.make_async_remote_copy(
            src_ref=fsend.at[kind, 0], dst_ref=rrecv.at[kind, z, me],
            send_sem=rf_send, recv_sem=rfar_recv.at[kind],
            device_id={"expert": far}, device_id_type=MESH,
        ).start()

        @pl.when(leftward)
        def _():
            arrived(nsum.at[kind, 0], n_recv.at[kind, 0])

        @pl.when(rightward)
        def _():
            arrived(nsum.at[kind, 1], n_recv.at[kind, 1])

        fsend[kind, 1] = (
            rsend[kind, z, far2].astype(f32)
            + jnp.where(leftward, nsum[kind, 0].astype(f32), 0.0)
            + jnp.where(rightward, nsum[kind, 1].astype(f32), 0.0)
        ).astype(bf16)
        pltpu.make_async_remote_copy(
            src_ref=fsend.at[kind, 1], dst_ref=rrecv.at[kind, z, me],
            send_sem=rf_send, recv_sem=rnext_recv.at[kind, z],
            device_id={"expert": far2}, device_id_type=MESH,
        ).start()

    def combine(kind, chunk):
        exchanged(rsend, rrecv, kind, chunk, r_recv, rloc_sem)

        @pl.when(jnp.logical_not(adjacent(chunk)))
        def _():
            arrived(rrecv.at[kind, chunk, far2], rnext_recv.at[kind, chunk])

        block = rrecv[kind, chunk].reshape(rows, cols)
        if kind == 1:
            own[1] = nn_dot(pick0[...] + pick1[...], block)
            return
        out0, out1 = nn_dot(pick0[...], block), nn_dot(pick1[...], block)
        dy = home[chunk, 1].astype(f32)
        s0 = jnp.sum(dy * out0, axis=1, keepdims=True)
        s1 = jnp.sum(dy * out1, axis=1, keepdims=True)
        pacc[...] += jnp.where(lane == 0, s0, 0.0) + jnp.where(lane == 1, s1, 0.0)
        own[0] = p0 * out0 + p1 * out1

    def add_in(kind, sum_in, sem):
        pltpu.make_async_copy(sum_in, sum_in, sem).wait()
        own[kind] += sum_in[...].astype(f32)

    def places(source, chunk):
        upward = chunk > source
        return upward, jnp.where(upward, source, parts - 1 - source) % 2 == 1

    def sum_on(kind, chunk):
        combine(kind, chunk)
        upward, joins = places(z, chunk)
        stops = jnp.logical_not(joins | adjacent(chunk))

        @pl.when(joins)
        def _():
            add_in(kind, joined.at[kind, chunk], j_recv.at[kind, chunk])

        part[kind, chunk] = own[kind].astype(bf16)

        @pl.when(stops)
        def _():
            pltpu.make_async_remote_copy(
                src_ref=part.at[kind, chunk], dst_ref=joined.at[kind, chunk],
                send_sem=s_send, recv_sem=j_recv.at[kind, chunk],
                device_id={"dp": jnp.where(upward, z + 1, z - 1)}, device_id_type=MESH,
            ).start()

        @pl.when(jnp.logical_not(stops))
        def _():
            pltpu.make_async_remote_copy(
                src_ref=part.at[kind, chunk], dst_ref=gathered.at[kind, z],
                send_sem=s_send, recv_sem=s_recv.at[kind, z],
                device_id={"dp": chunk}, device_id_type=MESH,
            ).start()

    def sum_own(kind):
        arrived(rrecv.at[kind, z, far], rfar_recv.at[kind])
        combine(kind, z)

        @pl.loop(1, parts)
        def _(n):
            source = nearest(parts - n)
            _, joins = places(source, z)

            @pl.when(joins | adjacent(source))
            def _():
                add_in(kind, gathered.at[kind, source], s_recv.at[kind, source])

        both_ref[kind] = own[kind].astype(bf16)

    load_g.wait()

    @pl.loop(0, parts)
    def _(n):
        contract(0, pre, wg, nearest(n))

    hid[...] = (pre[...] * jax.nn.sigmoid(pre[...])).astype(bf16)
    load_d.wait()
    split = parts // 2 + 1

    @pl.loop(1, split)
    def _(n):
        give_back(0, hid, wd, nearest(parts - n))

    @pl.loop(0, parts)
    def _(n):
        contract(1, back, wd, nearest(n))

    v = pre[...]
    sig = jax.nn.sigmoid(v)
    gterm[...] = (back[...] * sig * (1.0 + v * (1.0 - sig))).astype(bf16)

    @pl.loop(1, split)
    def _(n):
        give_back(1, gterm, wg, nearest(parts - n))

    @pl.loop(split, parts)
    def _(n):
        give_back(0, hid, wd, nearest(parts - n))
        give_back(1, gterm, wg, nearest(parts - n))

    give_own(0, hid, wd)
    give_own(1, gterm, wg)

    @pl.loop(1, split)
    def _(n):
        sum_on(0, nearest(parts - n))

    give_sums(0)

    @pl.loop(1, split)
    def _(n):
        sum_on(1, nearest(parts - n))

    give_sums(1)

    @pl.loop(split, parts)
    def _(n):
        sum_on(0, nearest(parts - n))
        sum_on(1, nearest(parts - n))

    sum_own(0)
    psend[...] = jnp.transpose(pacc[...])[0:8]

    @pl.loop(1, parts)
    def _(i):
        pltpu.make_async_remote_copy(
            src_ref=psend, dst_ref=precv.at[z],
            send_sem=p_send, recv_sem=p_recv,
            device_id={"dp": flip(z, i, parts)}, device_id_type=MESH,
        ).start()

    passed = home.at[z]

    @pl.when(rightward)
    def _():
        @pl.loop(0, z + 1)
        def _(i):
            pltpu.make_async_copy(passed, passed, ag_send).wait()

    @pl.when(leftward)
    def _():
        @pl.loop(0, parts - z)
        def _(i):
            pltpu.make_async_copy(passed, passed, ag_send).wait()

    several = send.at[0, 0, pl.ds(0, experts - 3)]
    others = part.at[0, pl.ds(0, parts - 1)]
    row = fsum.at[0]

    @pl.loop(0, 2)
    def _(kind):
        pltpu.make_async_copy(others, others, s_send).wait()

        @pl.loop(0, parts)
        def _(i):
            pltpu.make_async_copy(several, several, a_send).wait()
            pltpu.make_async_copy(several, several, r_send).wait()

        @pl.loop(0, 2)
        def _(i):
            pltpu.make_async_copy(row, row, f_send).wait()
            pltpu.make_async_copy(row, row, rf_send).wait()

    sum_own(1)

    rest = precv.at[pl.ds(0, parts - 1)]
    with jax.named_scope("prob_wait"):
        pltpu.make_async_copy(rest, rest, p_recv).wait()
    pg_ref[...] = psend[0:2]

    @pl.loop(1, parts)
    def _(i):
        pg_ref[...] += precv[flip(z, i, parts), 0:2]
    pltpu.make_async_copy(rest, rest, p_send).wait()


def split_kernel(both_ref, prob_ref, lo_ref, ig_ref, pg_ref):
    lo_ref[...] = both_ref[0]
    ig_ref[...] = both_ref[1]
    pg_ref[...] = prob_ref[...]


def per_device(inputs, out_grad, gate_probs, expert_ids, gate_proj, down_proj):
    parts = lax.axis_size("dp")
    experts = lax.axis_size("expert")
    tokens, cols = inputs.shape
    cap = -(-(3 * tokens // experts) // 16) * 16
    rows = experts * cap
    _, width, hidden = gate_proj.shape
    bf16, f32 = jnp.bfloat16, jnp.float32
    vmem = pl.BlockSpec(memory_space=pltpu.VMEM)
    hbm = pl.BlockSpec(memory_space=pl.ANY)
    dma = pltpu.SemaphoreType.DMA
    both, prob = pl.pallas_call(
        functools.partial(moe_kernel, parts, experts, cap),
        out_shape=(
            jax.ShapeDtypeStruct((2, tokens, cols), bf16),
            jax.ShapeDtypeStruct((2, tokens), f32),
        ),
        in_specs=[vmem, vmem, vmem, vmem, hbm, hbm],
        out_specs=(vmem, vmem),
        scratch_shapes=[
            pltpu.VMEM((hidden, width), bf16),
            pltpu.VMEM((hidden, width), bf16),
            pltpu.VMEM((parts, 2, tokens, cols), bf16),
            pltpu.VMEM((tokens, rows), bf16),
            pltpu.VMEM((tokens, rows), bf16),
            pltpu.VMEM((rows, tokens), bf16),
            pltpu.VMEM((rows, 1), f32),
            pltpu.VMEM((2, parts, experts, cap, cols), bf16),
            pltpu.VMEM((2, parts, experts, cap, cols), bf16),
            pltpu.VMEM((rows, hidden), f32),
            pltpu.VMEM((rows, hidden), f32),
            pltpu.VMEM((rows, hidden), bf16),
            pltpu.VMEM((rows, hidden), bf16),
            pltpu.VMEM((2, parts, experts, cap, cols), bf16),
            pltpu.VMEM((2, parts, experts, cap, cols), bf16),
            pltpu.VMEM((2, parts, tokens, cols), bf16),
            pltpu.VMEM((2, parts, tokens, cols), bf16),
            pltpu.VMEM((2, parts, tokens, cols), bf16),
            pltpu.VMEM((2, tokens, cols), f32),
            pltpu.VMEM((tokens, LANES), f32),
            pltpu.VMEM((8, tokens), f32),
            pltpu.VMEM((parts, 8, tokens), f32),
            pltpu.VMEM((2, parts, cap, cols), bf16),
            pltpu.VMEM((2, 2, cap, cols), bf16),
            pltpu.VMEM((2, 2, cap, cols), bf16),
            dma((2,)), dma, dma((2, parts)), dma((2, parts)), dma, dma((2, parts)),
            dma((2, parts)), dma((2, parts)),
            dma((2, parts)), dma, dma((2, parts)), dma((2,)), dma((2, parts)), dma, dma,
            dma, dma((2, parts)), dma((2, parts)), dma, dma, dma((2,)), dma((2, 2)),
        ],
        compiler_params=pltpu.CompilerParams(
            collective_id=0, has_side_effects=True, vmem_limit_bytes=56 * 1024 * 1024
        ),
    )(inputs, out_grad, gate_probs.T, expert_ids.T, jnp.swapaxes(gate_proj, 1, 2), down_proj)
    layer_out, in_grad, prob_grad = pl.pallas_call(
        split_kernel,
        out_shape=(
            jax.ShapeDtypeStruct((tokens, cols), bf16),
            jax.ShapeDtypeStruct((tokens, cols), bf16),
            jax.ShapeDtypeStruct((2, tokens), f32),
        ),
        in_specs=[vmem, vmem],
        out_specs=(vmem, vmem, vmem),
    )(both, prob)
    return layer_out, in_grad, prob_grad.T


def solution(mesh):
    placed = (
        P("expert", "dp"),
        P("expert", "dp"),
        P("expert", None),
        P("expert", None),
        P("expert", None, "dp"),
        P("expert", "dp", None),
    )
    return jax.shard_map(
        per_device,
        mesh=mesh,
        in_specs=placed,
        out_specs=(P("expert", "dp"), P("expert", "dp"), P("expert", None)),
        check_vma=False,
    )
```

```python
import functools

import jax
import jax.numpy as jnp
from jax import lax
from jax.experimental import pallas as pl
from jax.experimental.pallas import tpu as pltpu
from jax.sharding import PartitionSpec as P

MESH = pl.DeviceIdType.MESH
LANES = 128
ROUTED = (0,)
SUMMED = (0,)


def flip(a, b, size):
    out, bit = 0, 1
    while bit < size:
        out = out + ((a // bit + b // bit) % 2) * bit
        bit *= 2
    return out


def nt_dot(left, right):
    return lax.dot_general(
        left, right, (((1,), (1,)), ((), ())), preferred_element_type=jnp.float32
    )


def nn_dot(left, right):
    return jnp.dot(left, right, preferred_element_type=jnp.float32)


def moe_kernel(
    parts, experts, cap,
    x_ref, dy_ref, p_ref, id_ref, wg_hbm, wd_hbm,
    both_ref, pg_ref,
    wg, wd, home, pick0, pick1, spread, weight,
    send, recv, pre, back, hid, gterm, rsend, rrecv,
    part, gathered, joined, own, pacc, psend, precv, fsum, nsum, fsend,
    w_sem, ag_send, ag_recv, loc_sem, a_send, a_recv, far_recv, next_recv,
    rloc_sem, r_send, r_recv, rfar_recv, rnext_recv, f_send, rf_send,
    s_send, s_recv, j_recv, p_send, p_recv, h_recv, n_recv,
):
    z = lax.axis_index("dp")
    me = lax.axis_index("expert")
    far = flip(me, experts - 2, experts)
    far2 = flip(me, experts - 1, experts)
    tokens, cols = x_ref.shape
    rows = experts * cap
    bf16, f32 = jnp.bfloat16, jnp.float32
    rightward, leftward = z + 1 < parts, z > 0

    load_g = pltpu.make_async_copy(wg_hbm.at[0], wg, w_sem.at[0])
    load_d = pltpu.make_async_copy(wd_hbm.at[0], wd, w_sem.at[1])
    load_g.start()
    load_d.start()

    barrier = pltpu.get_barrier_semaphore()

    @pl.loop(1, parts)
    def _(i):
        pl.semaphore_signal(
            barrier, inc=1, device_id={"dp": flip(z, i, parts)}, device_id_type=MESH
        )

    @pl.loop(1, experts)
    def _(j):
        pl.semaphore_signal(
            barrier, inc=1, device_id={"expert": flip(me, j, experts)}, device_id_type=MESH
        )

    lowhalf = 2 * z < parts
    paired = 2 * jnp.where(lowhalf, z, parts - 1 - z)

    def nearest(n):
        near_by = z + (n + 1) // 2 * (1 - 2 * (n % 2))
        beyond = jnp.where(lowhalf, n, parts - 1 - n)
        return jnp.where(n <= paired, near_by, beyond)

    def adjacent(chunk):
        return (chunk - z) * (chunk - z) == 1

    def over_dp(kinds, kind, place, chunk):
        close = (chunk - place) * (chunk - place) == 1
        if kind in kinds:
            return close
        return close & (place > 0) & (place + 1 < parts)

    def routed(kind, place, chunk):
        return over_dp(ROUTED, kind, place, chunk)

    def summed(kind, place, chunk):
        return over_dp(SUMMED, kind, place, chunk)

    across = lax.broadcasted_iota(jnp.int32, (tokens, tokens), 1)
    down = lax.broadcasted_iota(jnp.int32, (tokens, tokens), 0)

    def column(row):
        return jnp.sum(jnp.where(across == down, row, 0), axis=1, keepdims=True)

    id0, id1 = column(id_ref[0:1, :]), column(id_ref[1:2, :])
    p0, p1 = column(p_ref[0:1, :]), column(p_ref[1:2, :])
    lane = lax.broadcasted_iota(jnp.int32, (tokens, LANES), 1)
    hot0 = (lane == id0).astype(f32)
    hot1 = (lane == id1).astype(f32)
    earlier = (across < down).astype(f32)
    count = nn_dot(earlier.astype(bf16), (hot0 + hot1).astype(bf16))
    pos0 = jnp.sum(count * hot0, axis=1, keepdims=True)
    pos1 = jnp.sum(count * hot1, axis=1, keepdims=True)
    slot = lax.broadcasted_iota(jnp.int32, (tokens, rows), 1)
    t0 = (slot == id0 * cap + pos0.astype(jnp.int32)).astype(f32)
    t1 = (slot == id1 * cap + pos1.astype(jnp.int32)).astype(f32)
    pick0[...] = t0.astype(bf16)
    pick1[...] = t1.astype(bf16)
    spread[...] = jnp.transpose(t0 + t1).astype(bf16)
    weight[...] = jnp.sum(jnp.transpose(t0 * p0 + t1 * p1), axis=1, keepdims=True)

    home[z, 0] = x_ref[...]
    home[z, 1] = dy_ref[...]
    with jax.named_scope("entry"):
        pl.semaphore_wait(barrier, parts - 1 + experts - 1)

    def pass_on(kind, chunk, neighbour):
        pltpu.make_async_remote_copy(
            src_ref=home.at[chunk, kind], dst_ref=home.at[chunk, kind],
            send_sem=ag_send, recv_sem=ag_recv.at[kind, chunk],
            device_id={"dp": neighbour}, device_id_type=MESH,
        ).start()

    @pl.when(rightward)
    def _():
        pass_on(0, z, z + 1)
        pass_on(1, z, z + 1)

    @pl.when(leftward)
    def _():
        pass_on(0, z, z - 1)
        pass_on(1, z, z - 1)

    def to_peer(source, target, kind, chunk, peer, send_sem, recv_sem):
        pltpu.make_async_remote_copy(
            src_ref=source.at[kind, chunk, peer], dst_ref=target.at[kind, chunk, me],
            send_sem=send_sem, recv_sem=recv_sem.at[kind, chunk],
            device_id={"expert": peer}, device_id_type=MESH,
        ).start()

    def exchange(source, target, kind, chunk, send_sem, recv_sem, local_sem):
        @pl.loop(3, experts)
        def _(j):
            to_peer(
                source, target, kind, chunk, flip(me, experts - j, experts), send_sem, recv_sem
            )

        pltpu.make_async_copy(
            source.at[kind, chunk, me], target.at[kind, chunk, me], local_sem.at[kind, chunk]
        ).start()

    def exchanged(source, target, kind, chunk, recv_sem, local_sem):
        pltpu.make_async_copy(
            source.at[kind, chunk, me], target.at[kind, chunk, me], local_sem.at[kind, chunk]
        ).wait()
        several = target.at[kind, chunk, pl.ds(0, experts - 3)]
        pltpu.make_async_copy(several, several, recv_sem.at[kind, chunk]).wait()

    def arrived(block, sem):
        pltpu.make_async_copy(block, block, sem).wait()

    def slot_rows(kind, chunk):
        picked = nn_dot(spread[...], home[chunk, kind])
        if kind == 1:
            picked = weight[...] * picked
        send[kind, chunk] = picked.astype(bf16).reshape(experts, cap, cols)

    def dispatch_own(kind):
        slot_rows(kind, z)
        to_peer(send, recv, kind, z, far, f_send, far_recv)
        to_peer(send, recv, kind, z, far2, f_send, next_recv)
        exchange(send, recv, kind, z, a_send, a_recv, loc_sem)

    def receive(kind, chunk):
        arrived(home.at[chunk, kind], ag_recv.at[kind, chunk])

        @pl.when((chunk < z) & rightward)
        def _():
            pass_on(kind, chunk, z + 1)

        @pl.when((chunk > z) & leftward)
        def _():
            pass_on(kind, chunk, z - 1)

    def dispatch(kind, chunk):
        slot_rows(kind, chunk)

        @pl.when(jnp.logical_not(routed(kind, z, chunk)))
        def _():
            to_peer(send, recv, kind, chunk, far2, f_send, next_recv)

        exchange(send, recv, kind, chunk, a_send, a_recv, loc_sem)

    def relay():
        for kind in (0, 1):
            arrived(recv.at[kind, z, far], far_recv.at[kind, z])
            arrived(recv.at[kind, z, far2], next_recv.at[kind, z])

        def onward(kind, peer, sem, chunk):
            pltpu.make_async_remote_copy(
                src_ref=recv.at[kind, z, peer], dst_ref=recv.at[kind, z, peer],
                send_sem=f_send, recv_sem=sem.at[kind, z],
                device_id={"dp": chunk}, device_id_type=MESH,
            ).start()

        for kind in (0, 1):

            @pl.loop(1, parts)
            def _(n):
                onward(kind, far, far_recv, nearest(parts - n))

            @pl.when(rightward & routed(kind, z + 1, z))
            def _():
                onward(kind, far2, next_recv, z + 1)

            @pl.when(leftward & routed(kind, z - 1, z))
            def _():
                onward(kind, far2, next_recv, z - 1)

    inner = rightward & leftward
    dispatch_own(0)
    dispatch_own(1)
    pre[...] = jnp.zeros_like(pre)
    back[...] = jnp.zeros_like(back)
    pacc[...] = jnp.zeros_like(pacc)

    @pl.loop(1, parts)
    def _(n):
        chunk = nearest(n)
        for kind in (0, 1):
            rrecv[kind, chunk, far] = jnp.zeros((cap, cols), bf16)

            @pl.when(summed(kind, z, chunk))
            def _():
                rrecv[kind, chunk, far2] = jnp.zeros((cap, cols), bf16)

    @pl.loop(1, parts)
    def _(i):
        lower, upper = z - i, z + i
        for kind in (0, 1):
            for step in (receive, dispatch):

                @pl.when(lower >= 0)
                def _():
                    step(kind, lower)

                @pl.when(upper < parts)
                def _():
                    step(kind, upper)

        @pl.when((i == 1) & jnp.logical_not(inner))
        def _():
            relay()

    @pl.when(inner)
    def _():
        relay()

    def contract(kind, total, w, chunk):
        start = pl.multiple_of(chunk * cols, cols)
        exchanged(send, recv, kind, chunk, a_recv, loc_sem)

        @pl.when(chunk != z)
        def _():
            arrived(recv.at[kind, chunk, far], far_recv.at[kind, chunk])
            arrived(recv.at[kind, chunk, far2], next_recv.at[kind, chunk])

        total[...] += nt_dot(recv[kind, chunk].reshape(rows, cols), w[:, pl.ds(start, cols)])

    def produce(kind, term, w, chunk):
        start = pl.multiple_of(chunk * cols, cols)
        rsend[kind, chunk] = (
            nn_dot(term[...], w[:, pl.ds(start, cols)]).astype(bf16).reshape(experts, cap, cols)
        )

    def give_back(kind, term, w, chunk):
        produce(kind, term, w, chunk)
        pltpu.make_async_remote_copy(
            src_ref=rsend.at[kind, chunk, far], dst_ref=fsum.at[kind, z],
            send_sem=rf_send, recv_sem=h_recv.at[kind],
            device_id={"dp": chunk}, device_id_type=MESH,
        ).start()

        def to_next(side):
            pltpu.make_async_remote_copy(
                src_ref=rsend.at[kind, chunk, far2], dst_ref=nsum.at[kind, side],
                send_sem=rf_send, recv_sem=n_recv.at[kind, side],
                device_id={"dp": chunk}, device_id_type=MESH,
            ).start()

        over = summed(kind, z, chunk)

        @pl.when(over & (chunk > z))
        def _():
            to_next(0)

        @pl.when(over & (chunk < z))
        def _():
            to_next(1)

        @pl.when(jnp.logical_not(over))
        def _():
            to_peer(rsend, rrecv, kind, chunk, far2, rf_send, rnext_recv)

        exchange(rsend, rrecv, kind, chunk, r_send, r_recv, rloc_sem)

    def give_own(kind, term, w):
        produce(kind, term, w, z)
        exchange(rsend, rrecv, kind, z, r_send, r_recv, rloc_sem)

    def give_sums(kind):
        sums = fsum.at[kind, pl.ds(0, parts - 1)]
        pltpu.make_async_copy(sums, sums, h_recv.at[kind]).wait()
        fsend[kind, 0] = lax.fori_loop(
            1, parts, lambda i, total: total + fsum[kind, flip(z, i, parts)].astype(f32),
            rsend[kind, z, far].astype(f32),
        ).astype(bf16)
        pltpu.make_async_remote_copy(
            src_ref=fsend.at[kind, 0], dst_ref=rrecv.at[kind, z, me],
            send_sem=rf_send, recv_sem=rfar_recv.at[kind],
            device_id={"expert": far}, device_id_type=MESH,
        ).start()

        below = leftward & summed(kind, z - 1, z)
        above = rightward & summed(kind, z + 1, z)

        @pl.when(below)
        def _():
            arrived(nsum.at[kind, 0], n_recv.at[kind, 0])

        @pl.when(above)
        def _():
            arrived(nsum.at[kind, 1], n_recv.at[kind, 1])

        fsend[kind, 1] = (
            rsend[kind, z, far2].astype(f32)
            + jnp.where(below, nsum[kind, 0].astype(f32), 0.0)
            + jnp.where(above, nsum[kind, 1].astype(f32), 0.0)
        ).astype(bf16)
        pltpu.make_async_remote_copy(
            src_ref=fsend.at[kind, 1], dst_ref=rrecv.at[kind, z, me],
            send_sem=rf_send, recv_sem=rnext_recv.at[kind, z],
            device_id={"expert": far2}, device_id_type=MESH,
        ).start()

    def combine(kind, chunk):
        exchanged(rsend, rrecv, kind, chunk, r_recv, rloc_sem)

        @pl.when(jnp.logical_not(summed(kind, z, chunk)))
        def _():
            arrived(rrecv.at[kind, chunk, far2], rnext_recv.at[kind, chunk])

        block = rrecv[kind, chunk].reshape(rows, cols)
        if kind == 1:
            own[1] = nn_dot(pick0[...] + pick1[...], block)
            return
        out0, out1 = nn_dot(pick0[...], block), nn_dot(pick1[...], block)
        dy = home[chunk, 1].astype(f32)
        s0 = jnp.sum(dy * out0, axis=1, keepdims=True)
        s1 = jnp.sum(dy * out1, axis=1, keepdims=True)
        pacc[...] += jnp.where(lane == 0, s0, 0.0) + jnp.where(lane == 1, s1, 0.0)
        own[0] = p0 * out0 + p1 * out1

    def add_in(kind, sum_in, sem):
        pltpu.make_async_copy(sum_in, sum_in, sem).wait()
        own[kind] += sum_in[...].astype(f32)

    def places(source, chunk):
        upward = chunk > source
        return upward, jnp.where(upward, source, parts - 1 - source) % 2 == 1

    def sum_on(kind, chunk):
        combine(kind, chunk)
        upward, joins = places(z, chunk)
        stops = jnp.logical_not(joins | adjacent(chunk))

        @pl.when(joins)
        def _():
            add_in(kind, joined.at[kind, chunk], j_recv.at[kind, chunk])

        part[kind, chunk] = own[kind].astype(bf16)

        @pl.when(stops)
        def _():
            pltpu.make_async_remote_copy(
                src_ref=part.at[kind, chunk], dst_ref=joined.at[kind, chunk],
                send_sem=s_send, recv_sem=j_recv.at[kind, chunk],
                device_id={"dp": jnp.where(upward, z + 1, z - 1)}, device_id_type=MESH,
            ).start()

        @pl.when(jnp.logical_not(stops))
        def _():
            pltpu.make_async_remote_copy(
                src_ref=part.at[kind, chunk], dst_ref=gathered.at[kind, z],
                send_sem=s_send, recv_sem=s_recv.at[kind, z],
                device_id={"dp": chunk}, device_id_type=MESH,
            ).start()

    def sum_own(kind):
        arrived(rrecv.at[kind, z, far], rfar_recv.at[kind])
        combine(kind, z)

        @pl.loop(1, parts)
        def _(n):
            source = nearest(parts - n)
            _, joins = places(source, z)

            @pl.when(joins | adjacent(source))
            def _():
                add_in(kind, gathered.at[kind, source], s_recv.at[kind, source])

        both_ref[kind] = own[kind].astype(bf16)

    load_g.wait()

    @pl.loop(0, parts)
    def _(n):
        contract(0, pre, wg, nearest(n))

    hid[...] = (pre[...] * jax.nn.sigmoid(pre[...])).astype(bf16)
    load_d.wait()
    split = parts // 2 + 1

    @pl.loop(1, split)
    def _(n):
        give_back(0, hid, wd, nearest(parts - n))

    @pl.loop(0, parts)
    def _(n):
        contract(1, back, wd, nearest(n))

    v = pre[...]
    sig = jax.nn.sigmoid(v)
    gterm[...] = (back[...] * sig * (1.0 + v * (1.0 - sig))).astype(bf16)

    @pl.loop(1, split)
    def _(n):
        give_back(1, gterm, wg, nearest(parts - n))

    @pl.loop(split, parts)
    def _(n):
        give_back(0, hid, wd, nearest(parts - n))
        give_back(1, gterm, wg, nearest(parts - n))

    give_own(0, hid, wd)
    give_own(1, gterm, wg)

    @pl.loop(1, split)
    def _(n):
        sum_on(0, nearest(parts - n))

    give_sums(0)

    @pl.loop(1, split)
    def _(n):
        sum_on(1, nearest(parts - n))

    give_sums(1)

    @pl.loop(split, parts)
    def _(n):
        sum_on(0, nearest(parts - n))
        sum_on(1, nearest(parts - n))

    sum_own(0)
    psend[...] = jnp.transpose(pacc[...])[0:8]

    @pl.loop(1, parts)
    def _(i):
        pltpu.make_async_remote_copy(
            src_ref=psend, dst_ref=precv.at[z],
            send_sem=p_send, recv_sem=p_recv,
            device_id={"dp": flip(z, i, parts)}, device_id_type=MESH,
        ).start()

    passed = home.at[z]

    @pl.when(rightward)
    def _():
        @pl.loop(0, z + 1)
        def _(i):
            pltpu.make_async_copy(passed, passed, ag_send).wait()

    @pl.when(leftward)
    def _():
        @pl.loop(0, parts - z)
        def _(i):
            pltpu.make_async_copy(passed, passed, ag_send).wait()

    several = send.at[0, 0, pl.ds(0, experts - 3)]
    others = part.at[0, pl.ds(0, parts - 1)]
    row = fsum.at[0]

    def left(condition, sem):
        @pl.when(condition)
        def _():
            arrived(nsum.at[0, 0], sem)

    for kind in (0, 1):
        arrived(row, f_send)
        arrived(row, rf_send)
        arrived(nsum.at[0, 0], f_send)
        arrived(nsum.at[0, 0], rf_send)

        @pl.loop(1, parts)
        def _(n):
            other = nearest(n)
            left(jnp.logical_not(routed(kind, z, other)), f_send)
            left(routed(kind, other, z), f_send)
            arrived(nsum.at[0, 0], rf_send)

    @pl.loop(0, 2)
    def _(kind):
        pltpu.make_async_copy(others, others, s_send).wait()

        @pl.loop(0, parts)
        def _(i):
            pltpu.make_async_copy(several, several, a_send).wait()
            pltpu.make_async_copy(several, several, r_send).wait()

    sum_own(1)

    rest = precv.at[pl.ds(0, parts - 1)]
    with jax.named_scope("prob_wait"):
        pltpu.make_async_copy(rest, rest, p_recv).wait()
    pg_ref[...] = psend[0:2]

    @pl.loop(1, parts)
    def _(i):
        pg_ref[...] += precv[flip(z, i, parts), 0:2]
    pltpu.make_async_copy(rest, rest, p_send).wait()


def split_kernel(both_ref, prob_ref, lo_ref, ig_ref, pg_ref):
    lo_ref[...] = both_ref[0]
    ig_ref[...] = both_ref[1]
    pg_ref[...] = prob_ref[...]


def per_device(inputs, out_grad, gate_probs, expert_ids, gate_proj, down_proj):
    parts = lax.axis_size("dp")
    experts = lax.axis_size("expert")
    tokens, cols = inputs.shape
    cap = -(-(3 * tokens // experts) // 16) * 16
    rows = experts * cap
    _, width, hidden = gate_proj.shape
    bf16, f32 = jnp.bfloat16, jnp.float32
    vmem = pl.BlockSpec(memory_space=pltpu.VMEM)
    hbm = pl.BlockSpec(memory_space=pl.ANY)
    dma = pltpu.SemaphoreType.DMA
    both, prob = pl.pallas_call(
        functools.partial(moe_kernel, parts, experts, cap),
        out_shape=(
            jax.ShapeDtypeStruct((2, tokens, cols), bf16),
            jax.ShapeDtypeStruct((2, tokens), f32),
        ),
        in_specs=[vmem, vmem, vmem, vmem, hbm, hbm],
        out_specs=(vmem, vmem),
        scratch_shapes=[
            pltpu.VMEM((hidden, width), bf16),
            pltpu.VMEM((hidden, width), bf16),
            pltpu.VMEM((parts, 2, tokens, cols), bf16),
            pltpu.VMEM((tokens, rows), bf16),
            pltpu.VMEM((tokens, rows), bf16),
            pltpu.VMEM((rows, tokens), bf16),
            pltpu.VMEM((rows, 1), f32),
            pltpu.VMEM((2, parts, experts, cap, cols), bf16),
            pltpu.VMEM((2, parts, experts, cap, cols), bf16),
            pltpu.VMEM((rows, hidden), f32),
            pltpu.VMEM((rows, hidden), f32),
            pltpu.VMEM((rows, hidden), bf16),
            pltpu.VMEM((rows, hidden), bf16),
            pltpu.VMEM((2, parts, experts, cap, cols), bf16),
            pltpu.VMEM((2, parts, experts, cap, cols), bf16),
            pltpu.VMEM((2, parts, tokens, cols), bf16),
            pltpu.VMEM((2, parts, tokens, cols), bf16),
            pltpu.VMEM((2, parts, tokens, cols), bf16),
            pltpu.VMEM((2, tokens, cols), f32),
            pltpu.VMEM((tokens, LANES), f32),
            pltpu.VMEM((8, tokens), f32),
            pltpu.VMEM((parts, 8, tokens), f32),
            pltpu.VMEM((2, parts, cap, cols), bf16),
            pltpu.VMEM((2, 2, cap, cols), bf16),
            pltpu.VMEM((2, 2, cap, cols), bf16),
            dma((2,)), dma, dma((2, parts)), dma((2, parts)), dma, dma((2, parts)),
            dma((2, parts)), dma((2, parts)),
            dma((2, parts)), dma, dma((2, parts)), dma((2,)), dma((2, parts)), dma, dma,
            dma, dma((2, parts)), dma((2, parts)), dma, dma, dma((2,)), dma((2, 2)),
        ],
        compiler_params=pltpu.CompilerParams(
            collective_id=0, has_side_effects=True, vmem_limit_bytes=56 * 1024 * 1024
        ),
    )(inputs, out_grad, gate_probs.T, expert_ids.T, jnp.swapaxes(gate_proj, 1, 2), down_proj)
    layer_out, in_grad, prob_grad = pl.pallas_call(
        split_kernel,
        out_shape=(
            jax.ShapeDtypeStruct((tokens, cols), bf16),
            jax.ShapeDtypeStruct((tokens, cols), bf16),
            jax.ShapeDtypeStruct((2, tokens), f32),
        ),
        in_specs=[vmem, vmem],
        out_specs=(vmem, vmem, vmem),
    )(both, prob)
    return layer_out, in_grad, prob_grad.T


def solution(mesh):
    placed = (
        P("expert", "dp"),
        P("expert", "dp"),
        P("expert", None),
        P("expert", None),
        P("expert", None, "dp"),
        P("expert", "dp", None),
    )
    return jax.shard_map(
        per_device,
        mesh=mesh,
        in_specs=placed,
        out_specs=(P("expert", "dp"), P("expert", "dp"), P("expert", None)),
        check_vma=False,
    )
```

```python
import functools

import jax
import jax.numpy as jnp
from jax import lax
from jax.experimental import pallas as pl
from jax.experimental.pallas import tpu as pltpu
from jax.sharding import PartitionSpec as P

MESH = pl.DeviceIdType.MESH
LANES = 128
ROUTED = (0,)
SUMMED = (0, 1)


def flip(a, b, size):
    out, bit = 0, 1
    while bit < size:
        out = out + ((a // bit + b // bit) % 2) * bit
        bit *= 2
    return out


def nt_dot(left, right):
    return lax.dot_general(
        left, right, (((1,), (1,)), ((), ())), preferred_element_type=jnp.float32
    )


def nn_dot(left, right):
    return jnp.dot(left, right, preferred_element_type=jnp.float32)


def moe_kernel(
    parts, experts, cap,
    x_ref, dy_ref, p_ref, id_ref, wg_hbm, wd_hbm,
    both_ref, pg_ref,
    wg, wd, home, pick0, pick1, spread, weight,
    send, recv, pre, back, hid, gterm, rsend, rrecv,
    part, gathered, joined, own, pacc, psend, precv, fsum, nsum, fsend,
    w_sem, ag_send, ag_recv, loc_sem, a_send, a_recv, far_recv, next_recv,
    rloc_sem, r_send, r_recv, rfar_recv, rnext_recv, f_send, rf_send,
    s_send, s_recv, j_recv, p_send, p_recv, h_recv, n_recv,
):
    z = lax.axis_index("dp")
    me = lax.axis_index("expert")
    far = flip(me, experts - 2, experts)
    far2 = flip(me, experts - 1, experts)
    tokens, cols = x_ref.shape
    rows = experts * cap
    bf16, f32 = jnp.bfloat16, jnp.float32
    rightward, leftward = z + 1 < parts, z > 0

    load_g = pltpu.make_async_copy(wg_hbm.at[0], wg, w_sem.at[0])
    load_d = pltpu.make_async_copy(wd_hbm.at[0], wd, w_sem.at[1])
    load_g.start()
    load_d.start()

    barrier = pltpu.get_barrier_semaphore()

    @pl.loop(1, parts)
    def _(i):
        pl.semaphore_signal(
            barrier, inc=1, device_id={"dp": flip(z, i, parts)}, device_id_type=MESH
        )

    @pl.loop(1, experts)
    def _(j):
        pl.semaphore_signal(
            barrier, inc=1, device_id={"expert": flip(me, j, experts)}, device_id_type=MESH
        )

    lowhalf = 2 * z < parts
    paired = 2 * jnp.where(lowhalf, z, parts - 1 - z)

    def nearest(n):
        near_by = z + (n + 1) // 2 * (1 - 2 * (n % 2))
        beyond = jnp.where(lowhalf, n, parts - 1 - n)
        return jnp.where(n <= paired, near_by, beyond)

    def adjacent(chunk):
        return (chunk - z) * (chunk - z) == 1

    def over_dp(kinds, kind, place, chunk):
        close = (chunk - place) * (chunk - place) == 1
        if kind in kinds:
            return close
        return close & (place > 0) & (place + 1 < parts)

    def routed(kind, place, chunk):
        return over_dp(ROUTED, kind, place, chunk)

    def summed(kind, place, chunk):
        return over_dp(SUMMED, kind, place, chunk)

    across = lax.broadcasted_iota(jnp.int32, (tokens, tokens), 1)
    down = lax.broadcasted_iota(jnp.int32, (tokens, tokens), 0)

    def column(row):
        return jnp.sum(jnp.where(across == down, row, 0), axis=1, keepdims=True)

    id0, id1 = column(id_ref[0:1, :]), column(id_ref[1:2, :])
    p0, p1 = column(p_ref[0:1, :]), column(p_ref[1:2, :])
    lane = lax.broadcasted_iota(jnp.int32, (tokens, LANES), 1)
    hot0 = (lane == id0).astype(f32)
    hot1 = (lane == id1).astype(f32)
    earlier = (across < down).astype(f32)
    count = nn_dot(earlier.astype(bf16), (hot0 + hot1).astype(bf16))
    pos0 = jnp.sum(count * hot0, axis=1, keepdims=True)
    pos1 = jnp.sum(count * hot1, axis=1, keepdims=True)
    slot = lax.broadcasted_iota(jnp.int32, (tokens, rows), 1)
    t0 = (slot == id0 * cap + pos0.astype(jnp.int32)).astype(f32)
    t1 = (slot == id1 * cap + pos1.astype(jnp.int32)).astype(f32)
    pick0[...] = t0.astype(bf16)
    pick1[...] = t1.astype(bf16)
    spread[...] = jnp.transpose(t0 + t1).astype(bf16)
    weight[...] = jnp.sum(jnp.transpose(t0 * p0 + t1 * p1), axis=1, keepdims=True)

    home[z, 0] = x_ref[...]
    home[z, 1] = dy_ref[...]
    with jax.named_scope("entry"):
        pl.semaphore_wait(barrier, parts - 1 + experts - 1)

    def pass_on(kind, chunk, neighbour):
        pltpu.make_async_remote_copy(
            src_ref=home.at[chunk, kind], dst_ref=home.at[chunk, kind],
            send_sem=ag_send, recv_sem=ag_recv.at[kind, chunk],
            device_id={"dp": neighbour}, device_id_type=MESH,
        ).start()

    @pl.when(rightward)
    def _():
        pass_on(0, z, z + 1)
        pass_on(1, z, z + 1)

    @pl.when(leftward)
    def _():
        pass_on(0, z, z - 1)
        pass_on(1, z, z - 1)

    def to_peer(source, target, kind, chunk, peer, send_sem, recv_sem):
        pltpu.make_async_remote_copy(
            src_ref=source.at[kind, chunk, peer], dst_ref=target.at[kind, chunk, me],
            send_sem=send_sem, recv_sem=recv_sem.at[kind, chunk],
            device_id={"expert": peer}, device_id_type=MESH,
        ).start()

    def exchange(source, target, kind, chunk, send_sem, recv_sem, local_sem):
        @pl.loop(3, experts)
        def _(j):
            to_peer(
                source, target, kind, chunk, flip(me, experts - j, experts), send_sem, recv_sem
            )

        pltpu.make_async_copy(
            source.at[kind, chunk, me], target.at[kind, chunk, me], local_sem.at[kind, chunk]
        ).start()

    def exchanged(source, target, kind, chunk, recv_sem, local_sem):
        pltpu.make_async_copy(
            source.at[kind, chunk, me], target.at[kind, chunk, me], local_sem.at[kind, chunk]
        ).wait()
        several = target.at[kind, chunk, pl.ds(0, experts - 3)]
        pltpu.make_async_copy(several, several, recv_sem.at[kind, chunk]).wait()

    def arrived(block, sem):
        pltpu.make_async_copy(block, block, sem).wait()

    def slot_rows(kind, chunk):
        picked = nn_dot(spread[...], home[chunk, kind])
        if kind == 1:
            picked = weight[...] * picked
        send[kind, chunk] = picked.astype(bf16).reshape(experts, cap, cols)

    def dispatch_own(kind):
        slot_rows(kind, z)
        to_peer(send, recv, kind, z, far, f_send, far_recv)
        to_peer(send, recv, kind, z, far2, f_send, next_recv)
        exchange(send, recv, kind, z, a_send, a_recv, loc_sem)

    def receive(kind, chunk):
        arrived(home.at[chunk, kind], ag_recv.at[kind, chunk])

        @pl.when((chunk < z) & rightward)
        def _():
            pass_on(kind, chunk, z + 1)

        @pl.when((chunk > z) & leftward)
        def _():
            pass_on(kind, chunk, z - 1)

    def dispatch(kind, chunk):
        slot_rows(kind, chunk)

        @pl.when(jnp.logical_not(routed(kind, z, chunk)))
        def _():
            to_peer(send, recv, kind, chunk, far2, f_send, next_recv)

        exchange(send, recv, kind, chunk, a_send, a_recv, loc_sem)

    def relay():
        for kind in (0, 1):
            arrived(recv.at[kind, z, far], far_recv.at[kind, z])
            arrived(recv.at[kind, z, far2], next_recv.at[kind, z])

        def onward(kind, peer, sem, chunk):
            pltpu.make_async_remote_copy(
                src_ref=recv.at[kind, z, peer], dst_ref=recv.at[kind, z, peer],
                send_sem=f_send, recv_sem=sem.at[kind, z],
                device_id={"dp": chunk}, device_id_type=MESH,
            ).start()

        for kind in (0, 1):

            @pl.loop(1, parts)
            def _(n):
                onward(kind, far, far_recv, nearest(parts - n))

            @pl.when(rightward & routed(kind, z + 1, z))
            def _():
                onward(kind, far2, next_recv, z + 1)

            @pl.when(leftward & routed(kind, z - 1, z))
            def _():
                onward(kind, far2, next_recv, z - 1)

    inner = rightward & leftward
    dispatch_own(0)
    dispatch_own(1)
    pre[...] = jnp.zeros_like(pre)
    back[...] = jnp.zeros_like(back)
    pacc[...] = jnp.zeros_like(pacc)

    @pl.loop(1, parts)
    def _(n):
        chunk = nearest(n)
        for kind in (0, 1):
            rrecv[kind, chunk, far] = jnp.zeros((cap, cols), bf16)

            @pl.when(summed(kind, z, chunk))
            def _():
                rrecv[kind, chunk, far2] = jnp.zeros((cap, cols), bf16)

    @pl.loop(1, parts)
    def _(i):
        lower, upper = z - i, z + i
        for kind in (0, 1):
            for step in (receive, dispatch):

                @pl.when(lower >= 0)
                def _():
                    step(kind, lower)

                @pl.when(upper < parts)
                def _():
                    step(kind, upper)

        @pl.when((i == 1) & jnp.logical_not(inner))
        def _():
            relay()

    @pl.when(inner)
    def _():
        relay()

    def contract(kind, total, w, chunk):
        start = pl.multiple_of(chunk * cols, cols)
        exchanged(send, recv, kind, chunk, a_recv, loc_sem)

        @pl.when(chunk != z)
        def _():
            arrived(recv.at[kind, chunk, far], far_recv.at[kind, chunk])
            arrived(recv.at[kind, chunk, far2], next_recv.at[kind, chunk])

        total[...] += nt_dot(recv[kind, chunk].reshape(rows, cols), w[:, pl.ds(start, cols)])

    def produce(kind, term, w, chunk):
        start = pl.multiple_of(chunk * cols, cols)
        rsend[kind, chunk] = (
            nn_dot(term[...], w[:, pl.ds(start, cols)]).astype(bf16).reshape(experts, cap, cols)
        )

    def give_back(kind, term, w, chunk):
        produce(kind, term, w, chunk)
        pltpu.make_async_remote_copy(
            src_ref=rsend.at[kind, chunk, far], dst_ref=fsum.at[kind, z],
            send_sem=rf_send, recv_sem=h_recv.at[kind],
            device_id={"dp": chunk}, device_id_type=MESH,
        ).start()

        def to_next(side):
            pltpu.make_async_remote_copy(
                src_ref=rsend.at[kind, chunk, far2], dst_ref=nsum.at[kind, side],
                send_sem=rf_send, recv_sem=n_recv.at[kind, side],
                device_id={"dp": chunk}, device_id_type=MESH,
            ).start()

        over = summed(kind, z, chunk)

        @pl.when(over & (chunk > z))
        def _():
            to_next(0)

        @pl.when(over & (chunk < z))
        def _():
            to_next(1)

        @pl.when(jnp.logical_not(over))
        def _():
            to_peer(rsend, rrecv, kind, chunk, far2, rf_send, rnext_recv)

        exchange(rsend, rrecv, kind, chunk, r_send, r_recv, rloc_sem)

    def give_own(kind, term, w):
        produce(kind, term, w, z)
        exchange(rsend, rrecv, kind, z, r_send, r_recv, rloc_sem)

    def give_sums(kind):
        sums = fsum.at[kind, pl.ds(0, parts - 1)]
        pltpu.make_async_copy(sums, sums, h_recv.at[kind]).wait()
        fsend[kind, 0] = lax.fori_loop(
            1, parts, lambda i, total: total + fsum[kind, flip(z, i, parts)].astype(f32),
            rsend[kind, z, far].astype(f32),
        ).astype(bf16)
        pltpu.make_async_remote_copy(
            src_ref=fsend.at[kind, 0], dst_ref=rrecv.at[kind, z, me],
            send_sem=rf_send, recv_sem=rfar_recv.at[kind],
            device_id={"expert": far}, device_id_type=MESH,
        ).start()

        below = leftward & summed(kind, z - 1, z)
        above = rightward & summed(kind, z + 1, z)

        @pl.when(below)
        def _():
            arrived(nsum.at[kind, 0], n_recv.at[kind, 0])

        @pl.when(above)
        def _():
            arrived(nsum.at[kind, 1], n_recv.at[kind, 1])

        fsend[kind, 1] = (
            rsend[kind, z, far2].astype(f32)
            + jnp.where(below, nsum[kind, 0].astype(f32), 0.0)
            + jnp.where(above, nsum[kind, 1].astype(f32), 0.0)
        ).astype(bf16)
        pltpu.make_async_remote_copy(
            src_ref=fsend.at[kind, 1], dst_ref=rrecv.at[kind, z, me],
            send_sem=rf_send, recv_sem=rnext_recv.at[kind, z],
            device_id={"expert": far2}, device_id_type=MESH,
        ).start()

    def combine(kind, chunk):
        exchanged(rsend, rrecv, kind, chunk, r_recv, rloc_sem)

        @pl.when(jnp.logical_not(summed(kind, z, chunk)))
        def _():
            arrived(rrecv.at[kind, chunk, far2], rnext_recv.at[kind, chunk])

        block = rrecv[kind, chunk].reshape(rows, cols)
        if kind == 1:
            own[1] = nn_dot(pick0[...] + pick1[...], block)
            return
        out0, out1 = nn_dot(pick0[...], block), nn_dot(pick1[...], block)
        dy = home[chunk, 1].astype(f32)
        s0 = jnp.sum(dy * out0, axis=1, keepdims=True)
        s1 = jnp.sum(dy * out1, axis=1, keepdims=True)
        pacc[...] += jnp.where(lane == 0, s0, 0.0) + jnp.where(lane == 1, s1, 0.0)
        own[0] = p0 * out0 + p1 * out1

    def add_in(kind, sum_in, sem):
        pltpu.make_async_copy(sum_in, sum_in, sem).wait()
        own[kind] += sum_in[...].astype(f32)

    def places(source, chunk):
        upward = chunk > source
        return upward, jnp.where(upward, source, parts - 1 - source) % 2 == 1

    def sum_on(kind, chunk):
        combine(kind, chunk)
        upward, joins = places(z, chunk)
        stops = jnp.logical_not(joins | adjacent(chunk))

        @pl.when(joins)
        def _():
            add_in(kind, joined.at[kind, chunk], j_recv.at[kind, chunk])

        part[kind, chunk] = own[kind].astype(bf16)

        @pl.when(stops)
        def _():
            pltpu.make_async_remote_copy(
                src_ref=part.at[kind, chunk], dst_ref=joined.at[kind, chunk],
                send_sem=s_send, recv_sem=j_recv.at[kind, chunk],
                device_id={"dp": jnp.where(upward, z + 1, z - 1)}, device_id_type=MESH,
            ).start()

        @pl.when(jnp.logical_not(stops))
        def _():
            pltpu.make_async_remote_copy(
                src_ref=part.at[kind, chunk], dst_ref=gathered.at[kind, z],
                send_sem=s_send, recv_sem=s_recv.at[kind, z],
                device_id={"dp": chunk}, device_id_type=MESH,
            ).start()

    def sum_own(kind):
        arrived(rrecv.at[kind, z, far], rfar_recv.at[kind])
        combine(kind, z)

        @pl.loop(1, parts)
        def _(n):
            source = nearest(parts - n)
            _, joins = places(source, z)

            @pl.when(joins | adjacent(source))
            def _():
                add_in(kind, gathered.at[kind, source], s_recv.at[kind, source])

        both_ref[kind] = own[kind].astype(bf16)

    load_g.wait()

    @pl.loop(0, parts)
    def _(n):
        contract(0, pre, wg, nearest(n))

    hid[...] = (pre[...] * jax.nn.sigmoid(pre[...])).astype(bf16)
    load_d.wait()
    split = parts // 2 + 1

    @pl.loop(1, split)
    def _(n):
        give_back(0, hid, wd, nearest(parts - n))

    @pl.loop(0, parts)
    def _(n):
        contract(1, back, wd, nearest(n))

    v = pre[...]
    sig = jax.nn.sigmoid(v)
    gterm[...] = (back[...] * sig * (1.0 + v * (1.0 - sig))).astype(bf16)

    @pl.loop(1, split)
    def _(n):
        give_back(1, gterm, wg, nearest(parts - n))

    @pl.loop(split, parts)
    def _(n):
        give_back(0, hid, wd, nearest(parts - n))
        give_back(1, gterm, wg, nearest(parts - n))

    give_own(0, hid, wd)
    give_own(1, gterm, wg)

    @pl.loop(1, split)
    def _(n):
        sum_on(0, nearest(parts - n))

    give_sums(0)

    @pl.loop(1, split)
    def _(n):
        sum_on(1, nearest(parts - n))

    give_sums(1)

    @pl.loop(split, parts)
    def _(n):
        sum_on(0, nearest(parts - n))
        sum_on(1, nearest(parts - n))

    sum_own(0)
    psend[...] = jnp.transpose(pacc[...])[0:8]

    @pl.loop(1, parts)
    def _(i):
        pltpu.make_async_remote_copy(
            src_ref=psend, dst_ref=precv.at[z],
            send_sem=p_send, recv_sem=p_recv,
            device_id={"dp": flip(z, i, parts)}, device_id_type=MESH,
        ).start()

    passed = home.at[z]

    @pl.when(rightward)
    def _():
        @pl.loop(0, z + 1)
        def _(i):
            pltpu.make_async_copy(passed, passed, ag_send).wait()

    @pl.when(leftward)
    def _():
        @pl.loop(0, parts - z)
        def _(i):
            pltpu.make_async_copy(passed, passed, ag_send).wait()

    several = send.at[0, 0, pl.ds(0, experts - 3)]
    others = part.at[0, pl.ds(0, parts - 1)]
    row = fsum.at[0]

    def left(condition, sem):
        @pl.when(condition)
        def _():
            arrived(nsum.at[0, 0], sem)

    for kind in (0, 1):
        arrived(row, f_send)
        arrived(row, rf_send)
        arrived(nsum.at[0, 0], f_send)
        arrived(nsum.at[0, 0], rf_send)

        @pl.loop(1, parts)
        def _(n):
            other = nearest(n)
            left(jnp.logical_not(routed(kind, z, other)), f_send)
            left(routed(kind, other, z), f_send)
            arrived(nsum.at[0, 0], rf_send)

    @pl.loop(0, 2)
    def _(kind):
        pltpu.make_async_copy(others, others, s_send).wait()

        @pl.loop(0, parts)
        def _(i):
            pltpu.make_async_copy(several, several, a_send).wait()
            pltpu.make_async_copy(several, several, r_send).wait()

    sum_own(1)

    rest = precv.at[pl.ds(0, parts - 1)]
    with jax.named_scope("prob_wait"):
        pltpu.make_async_copy(rest, rest, p_recv).wait()
    pg_ref[...] = psend[0:2]

    @pl.loop(1, parts)
    def _(i):
        pg_ref[...] += precv[flip(z, i, parts), 0:2]
    pltpu.make_async_copy(rest, rest, p_send).wait()


def split_kernel(both_ref, prob_ref, lo_ref, ig_ref, pg_ref):
    lo_ref[...] = both_ref[0]
    ig_ref[...] = both_ref[1]
    pg_ref[...] = prob_ref[...]


def per_device(inputs, out_grad, gate_probs, expert_ids, gate_proj, down_proj):
    parts = lax.axis_size("dp")
    experts = lax.axis_size("expert")
    tokens, cols = inputs.shape
    cap = -(-(3 * tokens // experts) // 16) * 16
    rows = experts * cap
    _, width, hidden = gate_proj.shape
    bf16, f32 = jnp.bfloat16, jnp.float32
    vmem = pl.BlockSpec(memory_space=pltpu.VMEM)
    hbm = pl.BlockSpec(memory_space=pl.ANY)
    dma = pltpu.SemaphoreType.DMA
    both, prob = pl.pallas_call(
        functools.partial(moe_kernel, parts, experts, cap),
        out_shape=(
            jax.ShapeDtypeStruct((2, tokens, cols), bf16),
            jax.ShapeDtypeStruct((2, tokens), f32),
        ),
        in_specs=[vmem, vmem, vmem, vmem, hbm, hbm],
        out_specs=(vmem, vmem),
        scratch_shapes=[
            pltpu.VMEM((hidden, width), bf16),
            pltpu.VMEM((hidden, width), bf16),
            pltpu.VMEM((parts, 2, tokens, cols), bf16),
            pltpu.VMEM((tokens, rows), bf16),
            pltpu.VMEM((tokens, rows), bf16),
            pltpu.VMEM((rows, tokens), bf16),
            pltpu.VMEM((rows, 1), f32),
            pltpu.VMEM((2, parts, experts, cap, cols), bf16),
            pltpu.VMEM((2, parts, experts, cap, cols), bf16),
            pltpu.VMEM((rows, hidden), f32),
            pltpu.VMEM((rows, hidden), f32),
            pltpu.VMEM((rows, hidden), bf16),
            pltpu.VMEM((rows, hidden), bf16),
            pltpu.VMEM((2, parts, experts, cap, cols), bf16),
            pltpu.VMEM((2, parts, experts, cap, cols), bf16),
            pltpu.VMEM((2, parts, tokens, cols), bf16),
            pltpu.VMEM((2, parts, tokens, cols), bf16),
            pltpu.VMEM((2, parts, tokens, cols), bf16),
            pltpu.VMEM((2, tokens, cols), f32),
            pltpu.VMEM((tokens, LANES), f32),
            pltpu.VMEM((8, tokens), f32),
            pltpu.VMEM((parts, 8, tokens), f32),
            pltpu.VMEM((2, parts, cap, cols), bf16),
            pltpu.VMEM((2, 2, cap, cols), bf16),
            pltpu.VMEM((2, 2, cap, cols), bf16),
            dma((2,)), dma, dma((2, parts)), dma((2, parts)), dma, dma((2, parts)),
            dma((2, parts)), dma((2, parts)),
            dma((2, parts)), dma, dma((2, parts)), dma((2,)), dma((2, parts)), dma, dma,
            dma, dma((2, parts)), dma((2, parts)), dma, dma, dma((2,)), dma((2, 2)),
        ],
        compiler_params=pltpu.CompilerParams(
            collective_id=0, has_side_effects=True, vmem_limit_bytes=56 * 1024 * 1024
        ),
    )(inputs, out_grad, gate_probs.T, expert_ids.T, jnp.swapaxes(gate_proj, 1, 2), down_proj)
    layer_out, in_grad, prob_grad = pl.pallas_call(
        split_kernel,
        out_shape=(
            jax.ShapeDtypeStruct((tokens, cols), bf16),
            jax.ShapeDtypeStruct((tokens, cols), bf16),
            jax.ShapeDtypeStruct((2, tokens), f32),
        ),
        in_specs=[vmem, vmem],
        out_specs=(vmem, vmem, vmem),
    )(both, prob)
    return layer_out, in_grad, prob_grad.T


def solution(mesh):
    placed = (
        P("expert", "dp"),
        P("expert", "dp"),
        P("expert", None),
        P("expert", None),
        P("expert", None, "dp"),
        P("expert", "dp", None),
    )
    return jax.shard_map(
        per_device,
        mesh=mesh,
        in_specs=placed,
        out_specs=(P("expert", "dp"), P("expert", "dp"), P("expert", None)),
        check_vma=False,
    )
```
